256 devices in a mesh: node: 64 (over z, y, core), feat: 4 (over x).
Axes of the slice: x: 4, y: 4, z: 8, core: 2. Of those that a mesh axis runs over, the one named last changes fastest.
Arguments:
- mesh_nodes: bfloat16 [16384, 512], P('node', 'feat'), may hold values from -6 to 6
- mesh_edges: bfloat16 [131072, 512], P(('node', 'feat')), may hold values from -6 to 6
- grid_nodes: bfloat16 [32768, 512], P('node', 'feat'), may hold values from -6 to 6
- m2g_edges: bfloat16 [98304, 512], P(('node', 'feat')), may hold values from -6 to 6
- edge_receivers: int32 [131072], P(('node', 'feat')), may hold values from 0 to 255
- edge_slots: int32 [131072], P(('node', 'feat')), may hold values from 0 to 1023
- send_rows: int32 [64, 64, 16], P('node'), may hold values from 0 to 255
- m2g_slots: int32 [98304], P(('node', 'feat')), may hold values from 0 to 1023
- m2g_send_rows: int32 [64, 64, 16], P('node'), may hold values from 0 to 255
- edge_w_in: bfloat16 [3, 3, 512, 512], replicated, may hold values from -0.15625 to 0.15625
- edge_w_out: bfloat16 [3, 512, 512], replicated, may hold values from -0.25 to 0.25
- edge_bias: float32 [3, 2, 512], replicated, may hold values from -2 to 2
- edge_gain: float32 [3, 512], replicated, may hold values from 0.5 to 1.5
- edge_shift: float32 [3, 512], replicated, may hold values from -2 to 2
- node_w_in: bfloat16 [3, 2, 512, 512], P(None, None, 'feat'), may hold values from -0.1875 to 0.1875
- node_w_out: bfloat16 [3, 512, 512], P(None, 'feat'), may hold values from -0.25 to 0.25
- node_bias: float32 [3, 2, 512], P(None, None, 'feat'), may hold values from -2 to 2
- node_gain: float32 [3, 512], P(None, 'feat'), may hold values from 0.5 to 1.5
- node_shift: float32 [3, 512], P(None, 'feat'), may hold values from -2 to 2
Outputs:
- grid_out: bfloat16 [32768, 512], P('node', 'feat')
The draws below stay inside these ranges and needn't reach their ends.
All inputs are finite; a program needn't handle non-finite values.
Results may differ from the reference program's by a relative error of at most 0.015.
Values may be sent and summed in bfloat16 or wider, within the bound.
No kernel may reach another device: no remote copies, remote signals or barrier semaphores. Data moves between devices by JAX's collectives and lax.ppermute only.
A program may use at most 64 MiB of HBM per device.

```python
import jax
import jax.numpy as jnp
from jax import lax

D = 512
NODE_DEV = 256
GRID_DEV = 512
LAYERS = 2
EDGE_DEV = 2048
M2G_DEV = 1536
BLOCK_BUF = 1024
SLOT = 16
M2G_BUF = 1024
M2G_SLOT = 16
NODES = 16384
EDGES = 131072
GRIDS = 32768
M2G_EDGES = 98304
N_NODE = 64


def touch_ends(drawn, stream_key, low, high):
    longest = drawn.shape.index(max(drawn.shape))
    spots = []
    for shift in (0, 1):
        where = [jax.random.randint(jax.random.fold_in(stream_key, axis), (), 0, length) for axis, length in enumerate(drawn.shape)]
        where[longest] = (where[longest] + shift) % drawn.shape[longest]
        spots.append(tuple(where))
    return drawn.at[spots[0]].set(low).at[spots[1]].set(high)


def block_levels(stream_key, extent, split, smallest, top_value):
    def one(dim, parts):
        steps = jax.random.uniform(jax.random.fold_in(jax.random.fold_in(stream_key, 6), dim), (parts,), jnp.float32, smallest / len(split), top_value / len(split))
        return jnp.repeat(jnp.exp(steps), extent[dim] // parts).reshape((-1,) + (1,) * (len(extent) - dim - 1))

    level = one(*split[0])
    for cut in split[1:]:
        level = level * one(*cut)
    return level


def centred(own_key, dims, scale, limit, shards=(), held_as=jnp.bfloat16):
    result = scale * jax.random.normal(own_key, dims, jnp.float32)
    if shards:
        result = result * block_levels(own_key, dims, shards, -0.22, 0.18)
    return jnp.clip(result, -limit, limit).astype(held_as)


def setup_inputs(seed: int = 0) -> dict:
    splits = jax.random.split(jax.random.key(seed), 20)
    return {
        "mesh_nodes": centred(splits[0], (NODES, D), 1.0, 6.0, ((0, 64), (1, 4))),
        "mesh_edges": centred(splits[1], (EDGES, D), 1.0, 6.0, ((0, 256),)),
        "grid_nodes": centred(splits[2], (GRIDS, D), 1.0, 6.0, ((0, 64), (1, 4))),
        "m2g_edges": centred(splits[3], (M2G_EDGES, D), 1.0, 6.0, ((0, 256),)),
        "edge_receivers": touch_ends(jax.random.randint(splits[4], (EDGES,), 0, NODE_DEV), jax.random.fold_in(splits[4], 1), 0, NODE_DEV - 1).astype(jnp.int32),
        "edge_slots": touch_ends(jax.random.randint(splits[5], (EDGES,), 0, BLOCK_BUF), jax.random.fold_in(splits[5], 1), 0, BLOCK_BUF - 1).astype(jnp.int32),
        "send_rows": touch_ends(jax.random.randint(splits[6], (N_NODE, N_NODE, SLOT), 0, NODE_DEV), jax.random.fold_in(splits[6], 1), 0, NODE_DEV - 1).astype(jnp.int32),
        "m2g_slots": touch_ends(jax.random.randint(splits[7], (M2G_EDGES,), 0, M2G_BUF), jax.random.fold_in(splits[7], 1), 0, M2G_BUF - 1).astype(jnp.int32),
        "m2g_send_rows": touch_ends(jax.random.randint(splits[8], (N_NODE, N_NODE, M2G_SLOT), 0, NODE_DEV), jax.random.fold_in(splits[8], 1), 0, NODE_DEV - 1).astype(jnp.int32),
        "edge_w_in": centred(splits[9], (LAYERS + 1, 3, D, D), (3 * D) ** -0.5, 0.15625),
        "edge_w_out": centred(splits[10], (LAYERS + 1, D, D), D ** -0.5, 0.25),
        "edge_bias": centred(splits[11], (LAYERS + 1, 2, D), 0.3, 2.0, (), jnp.float32),
        "edge_gain": jnp.clip(1.0 + 0.1 * jax.random.normal(splits[12], (LAYERS + 1, D), jnp.float32), 0.5, 1.5),
        "edge_shift": centred(splits[13], (LAYERS + 1, D), 0.3, 2.0, (), jnp.float32),
        "node_w_in": centred(splits[14], (LAYERS + 1, 2, D, D), (2 * D) ** -0.5, 0.1875, ((2, 4),)),
        "node_w_out": centred(splits[15], (LAYERS + 1, D, D), D ** -0.5, 0.25, ((1, 4),)),
        "node_bias": centred(splits[16], (LAYERS + 1, 2, D), 0.3, 2.0, ((2, 4),), jnp.float32),
        "node_gain": jnp.clip(1.0 + 0.1 * jax.random.normal(splits[17], (LAYERS + 1, D), jnp.float32), 0.5, 1.5),
        "node_shift": centred(splits[18], (LAYERS + 1, D), 0.3, 2.0, ((1, 4),), jnp.float32),
    }


EPSILON = 1e-05

def perceptron(inputs, weight_in, weight_out, bias_pair, gain_row, shift_row):
    hidden_pre = jnp.zeros((inputs[0].shape[0], weight_out.shape[1]), jnp.float32) + bias_pair[0].astype(jnp.float32)
    for term_index in range(len(inputs)):
        hidden_pre = hidden_pre + jnp.dot(inputs[term_index], weight_in[term_index], preferred_element_type=jnp.float32)
    hidden = jax.nn.silu(hidden_pre).astype(jnp.bfloat16)
    projected = jnp.dot(hidden, weight_out, preferred_element_type=jnp.float32) + bias_pair[1].astype(jnp.float32)
    mean_row = lax.optimization_barrier(jnp.mean(projected, axis=-1, keepdims=True))
    variance = lax.optimization_barrier(jnp.mean(projected * projected, axis=-1, keepdims=True)) - mean_row * mean_row
    normed = (projected - mean_row) * lax.rsqrt(variance + EPSILON) * gain_row + shift_row
    return (inputs[0].astype(jnp.float32) + normed).astype(jnp.bfloat16)

def reference(mesh_nodes, mesh_edges, grid_nodes, m2g_edges, edge_receivers, edge_slots, send_rows, m2g_slots, m2g_send_rows, edge_w_in, edge_w_out, edge_bias, edge_gain, edge_shift, node_w_in, node_w_out, node_bias, node_gain, node_shift):
    blocks = jnp.arange(N_NODE, dtype=jnp.int32)
    latent = mesh_nodes
    edge_latent = mesh_edges
    for layer_index in range(LAYERS):

        def edge_block(packed, latent=latent, layer_index=layer_index):
            block, block_edges, block_receivers, block_slots = packed
            source = (block_slots // SLOT).astype(jnp.int32)
            chosen = send_rows[source, block, block_slots % SLOT]
            senders = latent[source * NODE_DEV + chosen]
            receivers = latent[block * NODE_DEV + block_receivers]
            updated = perceptron((block_edges, senders, receivers), edge_w_in[layer_index], edge_w_out[layer_index], edge_bias[layer_index], edge_gain[layer_index], edge_shift[layer_index])
            summed = jax.ops.segment_sum(updated.astype(jnp.float32), block_receivers, num_segments=NODE_DEV)
            return (updated, summed.astype(jnp.bfloat16))
        edge_latent, summed = lax.map(edge_block, (blocks, edge_latent.reshape(N_NODE, EDGE_DEV, D), edge_receivers.reshape(N_NODE, EDGE_DEV), edge_slots.reshape(N_NODE, EDGE_DEV)))
        edge_latent = edge_latent.reshape(EDGES, D)
        summed = summed.reshape(NODES, D)
        latent = perceptron((latent, summed), node_w_in[layer_index], node_w_out[layer_index], node_bias[layer_index], node_gain[layer_index], node_shift[layer_index])

    def link_block(packed):
        block, block_links, block_cells, block_slots = packed
        source = (block_slots // M2G_SLOT).astype(jnp.int32)
        chosen = m2g_send_rows[source, block, block_slots % M2G_SLOT]
        senders = latent[source * NODE_DEV + chosen]
        receivers = jnp.broadcast_to(block_cells[:, None, :], (GRID_DEV, 3, D)).reshape(M2G_DEV, D)
        updated = perceptron((block_links, senders, receivers), edge_w_in[LAYERS], edge_w_out[LAYERS], edge_bias[LAYERS], edge_gain[LAYERS], edge_shift[LAYERS])
        return updated.astype(jnp.float32).reshape(GRID_DEV, 3, D).sum(axis=1).astype(jnp.bfloat16)
    grid_summed = lax.map(link_block, (blocks, m2g_edges.reshape(N_NODE, M2G_DEV, D), grid_nodes.reshape(N_NODE, GRID_DEV, D), m2g_slots.reshape(N_NODE, M2G_DEV)))
    grid_summed = grid_summed.reshape(GRIDS, D)
    return perceptron((grid_nodes, grid_summed), node_w_in[LAYERS], node_w_out[LAYERS], node_bias[LAYERS], node_gain[LAYERS], node_shift[LAYERS])
```

```python
import functools

import jax
import jax.numpy as jnp
from jax import lax
from jax.experimental import pallas as pl
from jax.experimental.pallas import tpu as pltpu
from jax.sharding import PartitionSpec as P

EPSILON = 1e-05
BF16 = jnp.bfloat16
F32 = jnp.float32


def call(body, outs, *args, scalars=1, flops=0, vmem=24):
    moved = sum(a.size * a.dtype.itemsize for a in (*args, *outs))
    specs = [pl.BlockSpec(memory_space=pltpu.SMEM)] * scalars
    specs += [pl.BlockSpec(memory_space=pltpu.VMEM)] * (len(args) - scalars)
    return pl.pallas_call(
        body,
        out_shape=outs,
        in_specs=specs,
        out_specs=[pl.BlockSpec(memory_space=pltpu.VMEM)] * len(outs),
        compiler_params=pltpu.CompilerParams(vmem_limit_bytes=vmem << 20),
        cost_estimate=pl.CostEstimate(flops=flops, bytes_accessed=moved, transcendentals=0),
    )(*args)


def shape(dims, dtype=BF16):
    return jax.ShapeDtypeStruct(dims, dtype)


def dot(a, b):
    return jnp.dot(a, b, preferred_element_type=F32)


def column_one_hot(index_row, width):
    count = index_row.shape[1]
    turned = jnp.broadcast_to(index_row, (128, count)).T
    lane = lax.broadcasted_iota(jnp.int32, (count, 128), 1)
    tiles = [
        jnp.where(turned == lane + base, 1.0, 0.0).astype(BF16) for base in range(0, width, 128)
    ]
    return jnp.concatenate(tiles, axis=1)


def owner_of(me, shift, size=4):
    return lax.rem(me + (size - shift), size)


def silu(v):
    half = 0.5 * v
    return half + half * jnp.tanh(half)


def layer_norm(v, gain, shift):
    mean = jnp.mean(v, axis=-1, keepdims=True)
    variance = jnp.mean(v * v, axis=-1, keepdims=True) - mean * mean
    return (v - mean) * lax.rsqrt(variance + EPSILON) * gain + shift


def first_gather(rows, nodes, out):
    out[...] = dot(column_one_hot(rows[...], nodes.shape[0]), nodes[...]).astype(BF16)


def index_body(slots, receivers, links, rows, link_rows, oh_s, oh_r, inc, oh_m, oh_o, oh_om):
    oh_s[...] = column_one_hot(slots[...], oh_s.shape[1])
    oh_r[...] = column_one_hot(receivers[...], oh_r.shape[1])
    oh_m[...] = column_one_hot(links[...], oh_m.shape[1])
    oh_o[...] = column_one_hot(rows[...], oh_o.shape[1])
    oh_om[...] = column_one_hot(link_rows[...], oh_om.shape[1])
    row = lax.broadcasted_iota(jnp.int32, inc.shape, 0)
    inc[...] = jnp.where(receivers[...] == row, 1.0, 0.0).astype(BF16)


def join_columns(me, *refs):
    *tiles, out = refs
    width = tiles[0].shape[1]
    for k, tile in enumerate(tiles):
        base = pl.multiple_of(owner_of(me[0], k) * width, width)
        out[:, pl.ds(base, width)] = tile[...]


def join_rows(me, *refs):
    *tiles, out = refs
    height = tiles[0].shape[0]
    for k, tile in enumerate(tiles):
        base = pl.multiple_of(owner_of(me[0], k) * height, height)
        out[pl.ds(base, height), :] = tile[...]


def weights_body(me, *refs):
    *tiles, out = refs
    part = tiles[0].shape[0] // 3
    for k, tile in enumerate(tiles):
        base = pl.multiple_of(owner_of(me[0], k) * part, part)
        for which in range(3):
            out[pl.ds(which * 4 * part + base, part), :] = tile[which * part : (which + 1) * part, :]


def edge_before(edge, one_hot, nodes, weight_edge, weight_receiver, bias, out):
    receivers = dot(one_hot[...], nodes[...]).astype(BF16)
    out[...] = (
        bias[0:1, :] + dot(edge[...], weight_edge[...]) + dot(receivers, weight_receiver[...])
    )


def edge_tail(before, one_hot, arrived, weight_sender, weight_out, bias, norm, edge):
    senders = dot(one_hot, arrived).astype(BF16)
    hidden = silu(before + dot(senders, weight_sender)).astype(BF16)
    projected = dot(hidden, weight_out) + bias[1:2, :]
    normed = layer_norm(projected, norm[0:1, :], norm[1:2, :])
    return (edge.astype(F32) + normed).astype(BF16)


def edge_after_split(
    me, before, one_hot, a0, a1, a2, a3, weight_sender, weight_out, bias, norm, edge, inc, new, part
):
    arrived = jnp.concatenate([a0[...], a1[...], a2[...], a3[...]], axis=1)
    width = a0.shape[1]
    turned = jnp.concatenate(
        [
            weight_sender[pl.ds(pl.multiple_of(owner_of(me[0], k) * width, width), width), :]
            for k in range(4)
        ],
        axis=0,
    )
    result = edge_tail(
        before[...], one_hot[...], arrived, turned, weight_out[...], bias, norm, edge[...]
    )
    new[...] = result
    part[...] = dot(inc[...], result).astype(BF16)


def edge_after(before, one_hot, arrived, weight_sender, weight_out, bias, norm, edge, inc, part):
    result = edge_tail(
        before[...],
        one_hot[...],
        arrived[...],
        weight_sender[...],
        weight_out[...],
        bias,
        norm,
        edge[...],
    )
    part[...] = dot(inc[...], result).astype(BF16)


def node_mlp(latent, summed, weights, table, layer):
    pre = table[2 * layer : 2 * layer + 1, :] + dot(latent, weights[0:512, :])
    pre = pre + dot(summed, weights[512:1024, :])
    hidden = silu(pre).astype(BF16)
    projected = dot(hidden, weights[1024:1536, :]) + table[2 * layer + 1 : 2 * layer + 2, :]
    normed = layer_norm(
        projected, table[6 + layer : 7 + layer, :], table[9 + layer : 10 + layer, :]
    )
    return (latent.astype(F32) + normed).astype(BF16)


def node_body(layer, p0, p1, p2, p3, latent, weights, table, one_hot, new, outgoing):
    summed = p0[...].astype(F32) + p1[...].astype(F32) + p2[...].astype(F32) + p3[...].astype(F32)
    result = node_mlp(latent[...], summed.astype(BF16), weights, table, layer)
    new[...] = result
    outgoing[...] = dot(one_hot[...], result).astype(BF16)


def link_before(me, edge, g0, g1, g2, g3, weight_edge, weight_cell, bias, out, cells):
    join_columns(me, g0, g1, g2, g3, cells)
    links, count = edge.shape[0], cells.shape[0]
    row = lax.broadcasted_iota(jnp.int32, (links, count), 0)
    first = 3 * lax.broadcasted_iota(jnp.int32, (links, count), 1)
    spread = jnp.where((row >= first) & (row < first + 3), 1.0, 0.0).astype(BF16)
    receivers = dot(spread, cells[...]).astype(BF16)
    out[...] = bias[0:1, :] + dot(edge[...], weight_edge[...]) + dot(receivers, weight_cell[...])


def link_after(
    layer,
    me,
    before,
    one_hot,
    arrived,
    weight_sender,
    weight_out,
    bias,
    norm,
    edge,
    cells,
    weights,
    table,
    o0,
    o1,
    o2,
    o3,
    whole,
):
    result = edge_tail(
        before[...],
        one_hot[...],
        arrived[...],
        weight_sender[...],
        weight_out[...],
        bias,
        norm,
        edge[...],
    )
    links, count = edge.shape[0], cells.shape[0]
    first = 3 * lax.broadcasted_iota(jnp.int32, (count, links), 0)
    column = lax.broadcasted_iota(jnp.int32, (count, links), 1)
    gather = jnp.where((column >= first) & (column < first + 3), 1.0, 0.0).astype(BF16)
    summed = dot(gather, result).astype(BF16)
    whole[...] = node_mlp(cells[...], summed, weights, table, layer)
    for k, out in enumerate((o0, o1, o2, o3)):
        base = pl.multiple_of(lax.rem(me[0] + k, 4) * 128, 128)
        out[...] = whole[:, pl.ds(base, 128)]


def moved(x, shift):
    size = lax.axis_size("feat")
    return lax.ppermute(x, "feat", [(i, (i + shift) % size) for i in range(size)])


def from_all(x):
    return [x, *(moved(x, k) for k in (1, 3, 2))]


def around(x):
    one, three, two = (moved(x, k) for k in (1, 3, 2))
    return [x, one, two, three]


def over_nodes(x):
    return lax.all_to_all(x, "node", split_axis=0, concat_axis=0, tiled=True)


def local(
    mesh_nodes,
    mesh_edges,
    grid_nodes,
    m2g_edges,
    edge_receivers,
    edge_slots,
    send_rows,
    m2g_slots,
    m2g_send_rows,
    edge_w_in,
    edge_w_out,
    edge_bias,
    edge_gain,
    edge_shift,
    node_w_in,
    node_w_out,
    node_bias,
    node_gain,
    node_shift,
):
    me = lax.axis_index("feat").astype(jnp.int32)
    who = me.reshape(1)
    nodes = mesh_nodes.shape[0]
    edges = mesh_edges.shape[0]
    links = m2g_edges.shape[0]
    blocks, slot = send_rows.shape[1:]
    slots = blocks * slot
    width = edge_w_out.shape[1]
    share = mesh_nodes.shape[1]
    cells = grid_nodes.shape[0] // 4

    rows = send_rows.reshape(1, slots)
    (outgoing,) = call(
        first_gather, [shape((slots, share))], rows, mesh_nodes, scalars=0, flops=2 * slots * nodes * share
    )
    arrived = over_nodes(outgoing.reshape(blocks, slot, share)).reshape(slots, share)

    mine = [
        jnp.concatenate([node_w_in[k].reshape(2 * share, width), node_w_out[k]]) for k in range(3)
    ]
    small = jnp.concatenate([node_bias.reshape(6, share), node_gain, node_shift])

    wide_tiles = around(mesh_nodes)
    small_tiles = around(small)
    grid_tiles = []
    for k in (0, 1, 3, 2):
        piece = lax.dynamic_slice_in_dim(grid_nodes, lax.rem(me + k, 4) * cells, cells, 0)
        grid_tiles.append(moved(piece, k) if k else piece)
    grid_tiles = [grid_tiles[0], grid_tiles[1], grid_tiles[3], grid_tiles[2]]
    mine_0 = around(mine[0])

    oh_s, oh_r, inc, oh_m, oh_o, oh_om = call(
        index_body,
        [
            shape((edges, slots)),
            shape((edges, nodes)),
            shape((nodes, edges)),
            shape((links, slots)),
            shape((slots, nodes)),
            shape((slots, nodes)),
        ],
        edge_slots.reshape(1, edges),
        edge_receivers.reshape(1, edges),
        m2g_slots.reshape(1, links),
        rows,
        m2g_send_rows.reshape(1, slots),
        scalars=0,
    )
    (latent,) = call(join_columns, [shape((nodes, width))], who, *wide_tiles)
    (table,) = call(join_columns, [shape((12, width), F32)], who, *small_tiles)
    norm = [jnp.stack([edge_gain[k], edge_shift[k]]) for k in range(3)]
    square = 2 * width * width

    def before(layer, edge, node):
        return call(
            edge_before,
            [shape((edges, width), F32)],
            edge,
            oh_r,
            node,
            edge_w_in[layer, 0],
            edge_w_in[layer, 2],
            edge_bias[layer],
            scalars=0,
            flops=2 * edges * square,
        )[0]

    def weights(tiles):
        return call(weights_body, [shape((3 * width, width))], who, *tiles)[0]

    def node(layer, part, latent, table, one_hot):
        parts = around(part)
        return call(
            functools.partial(node_body, layer),
            [shape((nodes, width)), shape((slots, width))],
            *parts,
            latent,
            mixed[layer],
            table,
            one_hot,
            scalars=0,
            flops=3 * nodes * square,
        )

    mixed = {0: weights(mine_0)}
    held = before(0, mesh_edges, latent)
    tiles = around(arrived)
    edge, part = call(
        edge_after_split,
        [shape((edges, width)), shape((nodes, width))],
        who,
        held,
        oh_s,
        *tiles,
        edge_w_in[0, 1],
        edge_w_out[0],
        edge_bias[0],
        norm[0],
        mesh_edges,
        inc,
        flops=4 * edges * square,
    )
    latent, outgoing = node(0, part, latent, table, oh_o)

    outgoing, mine_1 = lax.optimization_barrier((outgoing, mine[1]))
    arrived = over_nodes(outgoing.reshape(blocks, slot, width)).reshape(slots, width)
    mixed[1] = weights(around(mine_1))
    held = before(1, edge, latent)
    (part,) = call(
        edge_after,
        [shape((nodes, width))],
        held,
        oh_s,
        arrived,
        edge_w_in[1, 1],
        edge_w_out[1],
        edge_bias[1],
        norm[1],
        edge,
        inc,
        scalars=0,
        flops=4 * edges * square,
    )
    latent, outgoing = node(1, part, latent, table, oh_om)

    outgoing, mine_2 = lax.optimization_barrier((outgoing, mine[2]))
    arrived = over_nodes(outgoing.reshape(blocks, slot, width)).reshape(slots, width)
    mixed[2] = weights(around(mine_2))
    held, whole_cells = call(
        link_before,
        [shape((links, width), F32), shape((cells, width))],
        who,
        m2g_edges,
        *grid_tiles,
        edge_w_in[2, 0],
        edge_w_in[2, 2],
        edge_bias[2],
        flops=2 * links * square,
    )
    pieces = call(
        functools.partial(link_after, 2),
        [shape((cells, share))] * 4 + [shape((cells, width))],
        who,
        held,
        oh_m,
        arrived,
        edge_w_in[2, 1],
        edge_w_out[2],
        edge_bias[2],
        norm[2],
        m2g_edges,
        whole_cells,
        mixed[2],
        table,
        flops=4 * links * square,
    )
    back = [pieces[0], moved(pieces[1], 1), moved(pieces[2], 2), moved(pieces[3], 3)]
    return call(join_rows, [shape((4 * cells, share))], who, *back)[0]


def solution(mesh):
    in_specs = (
        P("node", "feat"),
        P(("node", "feat"), None),
        P("node", "feat"),
        P(("node", "feat"), None),
        P(("node", "feat")),
        P(("node", "feat")),
        P("node", None, None),
        P(("node", "feat")),
        P("node", None, None),
        P(),
        P(),
        P(),
        P(),
        P(),
        P(None, None, "feat", None),
        P(None, "feat", None),
        P(None, None, "feat"),
        P(None, "feat"),
        P(None, "feat"),
    )
    out_specs = P("node", "feat")
    return jax.shard_map(local, mesh=mesh, in_specs=in_specs, out_specs=out_specs, check_vma=False)
```

```python
import jax
import jax.numpy as jnp
from jax import lax
from jax.experimental import pallas as pl
from jax.experimental.pallas import tpu as pltpu
from jax.sharding import PartitionSpec as P


EPSILON = 1e-05
BF16 = jnp.bfloat16
F32 = jnp.float32

SMEM = pl.BlockSpec(memory_space=pltpu.SMEM)
VMEM = pl.BlockSpec(memory_space=pltpu.VMEM)
HBM = pl.BlockSpec(memory_space=pltpu.HBM)


class Fetched:
    def __init__(self, source, target, sem):
        self.copy = pltpu.make_async_copy(source, target, sem)
        self.copy.start()
        self.target = target

    def get(self):
        if self.copy is not None:
            self.copy.wait()
            self.copy = None
        return self.target


class Kept:
    def __init__(self, ref, target, sem):
        self.ref = ref
        self.copy = pltpu.make_async_copy(ref, target, sem)

    def put(self, value):
        self.ref[...] = value
        self.copy.start()


def block_of(ref, index):
    if not index:
        return ref
    return ref.at[tuple(i for i in index if not isinstance(i, tuple))]


def call(body, *, me=None, far=(), near=(), kept=(), outs=(), scratch=(), flops=0):
    far_arrays = []
    for array, _ in far:
        if not any(array is other for other in far_arrays):
            far_arrays.append(array)
    places = [next(k for k, other in enumerate(far_arrays) if other is array) for array, _ in far]
    blocks = [
        tuple(array.shape[len(index) :]) if all(isinstance(i, int) for i in index) else index[-1]
        for array, index in far
    ]
    scalars = [] if me is None else [me]
    counts = [len(scalars), len(far_arrays), len(near), len(kept), len(outs), len(far), len(kept)]

    def kernel(*refs):
        groups, at = [], 0
        for count in counts:
            groups.append(refs[at : at + count])
            at += count
        who, sources, near_refs, kept_refs, out_refs, buffers, kept_buffers = groups
        *extra, sems = refs[at:]
        fetched = [
            Fetched(block_of(sources[place], index), buffer, sems.at[k])
            for k, (place, (_, index), buffer) in enumerate(zip(places, far, buffers))
        ]
        holders = [
            Kept(buffer, target, sems.at[len(far) + k])
            for k, (buffer, target) in enumerate(zip(kept_buffers, kept_refs))
        ]
        body(*who, *fetched, *near_refs, *holders, *out_refs, *extra)
        for item in fetched:
            item.get()
        for item in holders:
            item.copy.wait()

    moved = sum(a.size * a.dtype.itemsize for a in (*near, *kept, *outs))
    moved += sum(2 * 512 * 512 for _ in far)
    fixed = [pltpu.with_memory_space_constraint(array, pltpu.HBM) for array in far_arrays]
    return pl.pallas_call(
        kernel,
        out_shape=[pltpu.HBM(k.shape, k.dtype) for k in kept] + list(outs),
        in_specs=[SMEM] * len(scalars) + [HBM] * len(fixed) + [VMEM] * len(near),
        out_specs=[HBM] * len(kept) + [VMEM] * len(outs),
        scratch_shapes=[
            pltpu.VMEM(block, array.dtype) for block, (array, _) in zip(blocks, far)
        ]
        + [pltpu.VMEM(k.shape, k.dtype) for k in kept]
        + list(scratch)
        + [pltpu.SemaphoreType.DMA((max(1, len(far) + len(kept)),))],
        compiler_params=pltpu.CompilerParams(vmem_limit_bytes=20 << 20),
        cost_estimate=pl.CostEstimate(flops=flops, bytes_accessed=moved, transcendentals=0),
    )(*scalars, *fixed, *near)


def shape(dims, dtype=BF16):
    return jax.ShapeDtypeStruct(dims, dtype)


def dot(a, b):
    return jnp.dot(a, b, preferred_element_type=F32)


def mask(condition):
    return jnp.where(condition, 1.0, 0.0).astype(BF16)


def column_one_hot(index_row, out):
    count = index_row.shape[1]
    turned = jnp.broadcast_to(index_row, (128, count)).T
    lane = lax.broadcasted_iota(jnp.int32, (count, 128), 1)
    for base in range(0, out.shape[1], 128):
        out[:, base : base + 128] = mask(turned == lane + base)


def table_one_hot(table, out):
    slot, blocks = table.shape
    lane = lax.broadcasted_iota(jnp.int32, (slot, out.shape[1]), 1)
    whole = table[...]
    for block in range(blocks):
        out[block * slot : (block + 1) * slot, :] = mask(whole[:, block : block + 1] == lane)


def row_one_hot(index_row, out):
    out[...] = mask(index_row == lax.broadcasted_iota(jnp.int32, out.shape, 0))


def owner(me, shift):
    return lax.rem(me[0] + (4 - shift), 4)


def lanes(index):
    return pl.ds(pl.multiple_of(index * 128, 128), 128)


def rows_at(index, height):
    return pl.ds(pl.multiple_of(index * height, height), height)


def silu(v):
    half = 0.5 * v
    return half + half * jnp.tanh(half)


def layer_norm(v, gain, shift):
    mean = jnp.mean(v, axis=-1, keepdims=True)
    variance = jnp.mean(v * v, axis=-1, keepdims=True) - mean * mean
    return (v - mean) * lax.rsqrt(variance + EPSILON) * gain + shift


def first_gather(table, nodes, out, one_hot):
    table_one_hot(table, one_hot)
    out[...] = dot(one_hot[...], nodes[...]).astype(BF16)


def setup_kernel(me, w_in, w_out, bias, gain, shift, grid, *refs):
    outs, (first, last, cells, small, sems) = refs[:8], refs[8:]
    part = w_out.shape[1]
    pairs = [(grid, cells)]
    for k in range(3):
        target, base = (first, 3 * part * k) if k < 2 else (last, 0)
        for row in range(2):
            pairs.append((w_in.at[k, row], target.at[pl.ds(base + row * part, part)]))
        pairs.append((w_out.at[k], target.at[pl.ds(base + 2 * part, part)]))
    loads = [pltpu.make_async_copy(a, b, sems.at[n]) for n, (a, b) in enumerate(pairs)]
    for load in loads:
        load.start()
    small[...] = jnp.zeros_like(small)
    for k in range(3):
        small[2 * k : 2 * k + 2, :] = bias[k]
    small[6:9, :] = gain[...]
    small[9:12, :] = shift[...]
    rest = small[...]
    tail = 6 * part
    first[tail:, :] = jnp.zeros((first.shape[0] - tail, first.shape[1]), BF16)
    for plane in range(3):
        piece = rest.astype(BF16)
        first[tail : tail + 16, plane * part : (plane + 1) * part] = piece
        rest = rest - piece.astype(F32)
    for load in loads:
        load.wait()
    half, height = first.shape[0] // 2, cells.shape[0] // 4
    pairs = [(first, outs[0]), (first.at[rows_at(me[1], half)], outs[1])]
    pairs += [(last, outs[2]), (last.at[rows_at(me[1], last.shape[0] // 2)], outs[3])]
    for k in range(4):
        pairs.append((cells.at[rows_at(lax.rem(me[0] + k, 4), height)], outs[4 + k]))
    stores = [pltpu.make_async_copy(a, b, sems.at[n]) for n, (a, b) in enumerate(pairs)]
    for store in stores:
        store.start()
    for store in stores:
        store.wait()


def setup(who, w_in, w_out, bias, gain, shift, grid):
    share, width = w_out.shape[1:]
    first, last = 6 * share + 32, 3 * share
    heights = [first, first // 2, last, last // 2]
    return pl.pallas_call(
        setup_kernel,
        out_shape=[pltpu.HBM((h, width), BF16) for h in heights]
        + [pltpu.HBM((grid.shape[0] // 4, share), BF16)] * 4,
        in_specs=[SMEM, HBM, HBM, VMEM, VMEM, VMEM, HBM],
        out_specs=[HBM] * 8,
        scratch_shapes=[
            pltpu.VMEM((first, width), BF16),
            pltpu.VMEM((last, width), BF16),
            pltpu.VMEM(grid.shape, BF16),
            pltpu.VMEM((16, share), F32),
            pltpu.SemaphoreType.DMA((10,)),
        ],
        name="setup",
        compiler_params=pltpu.CompilerParams(vmem_limit_bytes=20 << 20),
        cost_estimate=pl.CostEstimate(flops=0, bytes_accessed=4 << 20, transcendentals=0),
    )(
        who,
        pltpu.with_memory_space_constraint(w_in, pltpu.HBM),
        pltpu.with_memory_space_constraint(w_out, pltpu.HBM),
        bias,
        gain,
        shift,
        pltpu.with_memory_space_constraint(grid, pltpu.HBM),
    )


def placed(me, tiles, far, outs):
    mine, near, other, half, other_half = tiles
    height, first = half.shape[0], 1 + 2 * me[1]
    far[rows_at(me[1], height), :] = half[...]
    far[rows_at(1 - me[1], height), :] = other_half[...]
    owned = [(mine, 0), (near, first), (other, 4 - first), (far, 2)]
    owned = [(tile, lax.rem(me[0] + (4 - shift), 4)) for tile, shift in owned]
    for tile, base in owned:
        for layer, out in enumerate(outs):
            for part in range(3):
                row = (3 * layer + part) * 128
                out.ref[pl.ds(pl.multiple_of(part * 512 + base * 128, 128), 128), :] = tile[
                    row : row + 128, :
                ]
    for out in outs:
        out.copy.start()
    return owned


def weights_first(me, mine, near, other, half, other_half, one, two, table, far):
    owned = placed(me, (mine, near, other, half, other_half), far, (one, two))
    for tile, base in owned:
        planes = [tile[768:784, k * 128 : (k + 1) * 128].astype(F32) for k in range(3)]
        table.ref[:, lanes(base)] = planes[0] + planes[1] + planes[2]
    table.copy.start()


def weights_last(me, mine, near, other, half, other_half, out, far):
    placed(me, (mine, near, other, half, other_half), far, (out,))


def before_first(
    me, w_e, w_r, bias, n0, n1, n2, n3, edge, slots, receivers, rows, nodes, out, oh_s, inc, oh_o, oh_r
):
    for k, tile in enumerate((n0, n1, n2, n3)):
        nodes.ref[:, lanes(owner(me, k))] = tile[...]
    nodes.copy.start()
    column_one_hot(receivers[...], oh_r)
    taken = dot(oh_r[...], nodes.ref[...]).astype(BF16)
    total = dot(edge[...], w_e.get()[...])
    out[...] = total + dot(taken, w_r.get()[...]) + bias.get()[0, 0:1, :]
    column_one_hot(slots[...], oh_s)
    row_one_hot(receivers[...], inc)
    table_one_hot(rows, oh_o)


def before_second(
    w_e,
    w_r,
    edge,
    senders,
    latent_w,
    table,
    bias,
    nodes,
    slots,
    receivers,
    rows,
    out,
    sender_pre,
    oh_s,
    inc,
    oh_o,
    oh_r,
):
    column_one_hot(receivers[...], oh_r)
    taken = dot(oh_r[...], nodes[...]).astype(BF16)
    total = dot(edge.get()[...], w_e.get()[...])
    out[...] = total + dot(taken, w_r.get()[...]) + bias.get()[1, 0:1, :]
    sender_pre[...] = table.get()[0:1, :] + dot(senders.get()[...], latent_w.get()[0:512, :])
    column_one_hot(slots[...], oh_s)
    row_one_hot(receivers[...], inc)
    table_one_hot(rows, oh_o)


def before_links(me, w_e, w_r, bias, edge, g0, g1, g2, g3, slots, out, cells, oh_m):
    for k, tile in enumerate((g0, g1, g2, g3)):
        cells[:, lanes(owner(me, k))] = tile[...]
    links, count = edge.shape[0], cells.shape[0]
    row = lax.broadcasted_iota(jnp.int32, (links, count), 0)
    first = 3 * lax.broadcasted_iota(jnp.int32, (links, count), 1)
    spread = mask((row >= first) & (row < first + 3))
    taken = dot(spread, cells[...]).astype(BF16)
    total = dot(edge[...], w_e.get()[...])
    out[...] = total + dot(taken, w_r.get()[...]) + bias.get()[2, 0:1, :]
    column_one_hot(slots[...], oh_m)


def gathered_rows(me, one_hot, tiles, out):
    arrived = jnp.concatenate([tile[...] for tile in tiles], axis=1)
    rows = dot(one_hot[...], arrived).astype(BF16)
    for k in range(4):
        out[:, lanes(owner(me, k))] = rows[:, k * 128 : (k + 1) * 128]


def edge_tail(layer, before, senders, w_s, w_o, bias, gain, shift, edge):
    hidden = silu(before[...] + dot(senders, w_s.get()[...])).astype(BF16)
    projected = dot(hidden, w_o.get()[...]) + bias.get()[layer, 1:2, :]
    scale, offset = gain.get()[layer : layer + 1, :], shift.get()[layer : layer + 1, :]
    return (edge.astype(F32) + layer_norm(projected, scale, offset)).astype(BF16)


def node_tail(layer, latent, pre, summed, mixed, table, base=512):
    hidden = silu(pre + dot(summed, mixed[base : base + 512, :])).astype(BF16)
    projected = dot(hidden, mixed[base + 512 : base + 1024, :]) + table[2 * layer + 1 : 2 * layer + 2, :]
    normed = layer_norm(
        projected, table[6 + layer : 7 + layer, :], table[9 + layer : 10 + layer, :]
    )
    return (latent.astype(F32) + normed).astype(BF16)


def after_first(
    me,
    w_s,
    w_o,
    bias,
    gain,
    shift,
    before,
    one_hot,
    a0,
    a1,
    a2,
    a3,
    edge,
    inc,
    new,
    senders,
    p0,
    p1,
    p2,
    p3,
    held,
):
    gathered_rows(me, one_hot, (a0, a1, a2, a3), senders.ref)
    senders.copy.start()
    result = edge_tail(0, before, senders.ref[...], w_s, w_o, bias, gain, shift, edge[...])
    new.put(result)
    held[...] = dot(inc[...], result).astype(BF16)
    for k, out in enumerate((p0, p1, p2, p3)):
        out[...] = held[:, lanes(lax.rem(me[0] + k, 4))]


def after_second(
    me,
    w_s,
    w_o,
    bias,
    gain,
    shift,
    edge,
    senders,
    mixed,
    table,
    before,
    sender_pre,
    one_hot,
    a0,
    a1,
    a2,
    a3,
    inc,
    part,
    summed,
):
    gathered_rows(me, one_hot, (a0, a1, a2, a3), summed)
    latest = node_tail(
        0, senders.get()[...], sender_pre[...], summed[...], mixed.get(), table.get(), 0
    )
    result = edge_tail(1, before, latest, w_s, w_o, bias, gain, shift, edge.get()[...])
    part[...] = dot(inc[...], result).astype(BF16)


def after_links(
    me,
    w_s,
    w_o,
    bias,
    gain,
    shift,
    mixed,
    table,
    before,
    one_hot,
    a0,
    a1,
    a2,
    a3,
    edge,
    cells,
    o0,
    o1,
    o2,
    o3,
    senders,
    held,
):
    gathered_rows(me, one_hot, (a0, a1, a2, a3), senders)
    result = edge_tail(2, before, senders[...], w_s, w_o, bias, gain, shift, edge[...])
    links, count = edge.shape[0], cells.shape[0]
    first = 3 * lax.broadcasted_iota(jnp.int32, (count, links), 0)
    column = lax.broadcasted_iota(jnp.int32, (count, links), 1)
    added = dot(mask((column >= first) & (column < first + 3)), result).astype(BF16)
    weights, rows = mixed.get(), table.get()
    pre = rows[4:5, :] + dot(cells[...], weights[0:512, :])
    held[...] = node_tail(2, cells[...], pre, added, weights, rows)
    for k, out in enumerate((o0, o1, o2, o3)):
        out[...] = held[:, lanes(lax.rem(me[0] + k, 4))]


def sum_body(s0, s1, s2, s3, one_hot, summed, outgoing):
    total = s0[...].astype(F32) + s1[...].astype(F32) + s2[...].astype(F32) + s3[...].astype(F32)
    summed[...] = total.astype(BF16)
    outgoing[...] = dot(one_hot[...], summed[...]).astype(BF16)


def node_first(me, latent, mixed, table, s0, s1, s2, s3, new, summed):
    for k, tile in enumerate((s0, s1, s2, s3)):
        summed[:, lanes(owner(me, k))] = tile[...]
    old, weights, rows = latent.get()[...], mixed.get(), table.get()
    pre = rows[0:1, :] + dot(old, weights[0:512, :])
    new[...] = node_tail(0, old, pre, summed[...], weights, rows)


def node_second(me, mixed, table, latent, p0, p1, p2, p3, one_hot, outgoing, new):
    total = p0[...].astype(F32) + p1[...].astype(F32) + p2[...].astype(F32) + p3[...].astype(F32)
    old, weights, rows = latent[...], mixed.get(), table.get()
    pre = rows[2:3, :] + dot(old, weights[0:512, :])
    new[...] = node_tail(1, old, pre, total.astype(BF16), weights, rows)
    outgoing[...] = dot(one_hot[...], new[:, lanes(me[0])]).astype(BF16)


def join_body(me, r0, r1, r2, r3, out):
    for k, tile in enumerate((r0, r1, r2, r3)):
        out[rows_at(owner(me, k), 128), :] = tile[...]


def moved(x, shift):
    return lax.ppermute(x, "feat", [(i, (i + shift) % 4) for i in range(4)])


def around(x):
    one, three, two = (moved(x, k) for k in (1, 3, 2))
    return [x, one, two, three]


def handed(pieces):
    one, three, two = (moved(pieces[k], k) for k in (1, 3, 2))
    return [pieces[0], one, two, three]


def from_neighbours(whole, half):
    size = lax.axis_size("node")
    ring = [
        (n * 4 + f, n * 4 + (f + (1 if n % 2 == 0 else 3)) % 4) for n in range(size) for f in range(4)
    ]
    return lax.ppermute(whole, ("node", "feat"), ring), moved(half, 2)


def from_twin(x):
    return lax.ppermute(x, "node", [(n, n ^ 1) for n in range(lax.axis_size("node"))])


def over_nodes(x, blocks):
    tiles = x.reshape(blocks, x.shape[0] // blocks, x.shape[1])
    return lax.all_to_all(tiles, "node", split_axis=0, concat_axis=0, tiled=True).reshape(x.shape)


together = lax.optimization_barrier


def local(
    mesh_nodes,
    mesh_edges,
    grid_nodes,
    m2g_edges,
    edge_receivers,
    edge_slots,
    send_rows,
    m2g_slots,
    m2g_send_rows,
    edge_w_in,
    edge_w_out,
    edge_bias,
    edge_gain,
    edge_shift,
    node_w_in,
    node_w_out,
    node_bias,
    node_gain,
    node_shift,
):
    who = jnp.stack([lax.axis_index("feat"), lax.rem(lax.axis_index("node"), 2)]).astype(jnp.int32)
    nodes, share = mesh_nodes.shape
    edges, width = mesh_edges.shape
    links = m2g_edges.shape[0]
    blocks, slot = send_rows.shape[1:]
    slots = blocks * slot
    cells = grid_nodes.shape[0] // 4
    square = 2 * width * width
    rows, link_rows = send_rows[0].T, m2g_send_rows[0].T
    norms = [(edge_bias, ()), (edge_gain, ()), (edge_shift, ())]
    slot_row, receiver_row = edge_slots.reshape(1, edges), edge_receivers.reshape(1, edges)

    (outgoing,) = call(
        first_gather,
        near=[rows, mesh_nodes],
        outs=[shape((slots, share))],
        scratch=[pltpu.VMEM((slots, nodes), BF16)],
    )
    outgoing, late_nodes, late_who = together((outgoing, mesh_nodes, who))
    arrived = over_nodes(outgoing, blocks)
    node_tiles = around(late_nodes)
    prepared = setup(late_who, node_w_in, node_w_out, node_bias, node_gain, node_shift, grid_nodes)
    whole, half, whole_2, half_2, *grid_pieces = prepared
    arrived, half = together((arrived, half))
    tiles = around(arrived)
    latent, held, oh_s, inc, oh_o = call(
        before_first,
        me=who,
        far=[(edge_w_in, (0, 0)), (edge_w_in, (0, 2)), (edge_bias, ())],
        near=[*node_tiles, mesh_edges, slot_row, receiver_row, rows],
        kept=[shape((nodes, width))],
        outs=[
            shape((edges, width), F32),
            shape((edges, slots)),
            shape((nodes, edges)),
            shape((slots, nodes)),
        ],
        scratch=[pltpu.VMEM((edges, nodes), BF16)],
        flops=2 * edges * square,
    )
    edge, senders, *partial = call(
        after_first,
        me=who,
        far=[(edge_w_in, (0, 1)), (edge_w_out, (0,)), *norms],
        near=[held, oh_s, *tiles, mesh_edges, inc],
        kept=[shape((edges, width)), shape((edges, width))],
        outs=[shape((nodes, share))] * 4,
        scratch=[pltpu.VMEM((nodes, width), BF16)],
        flops=4 * edges * square,
    )
    *partial, whole, half = together((*partial, whole, half))
    sums = handed(partial)
    near, far = from_neighbours(whole, half)
    summed, outgoing = call(
        sum_body,
        near=[*sums, oh_o],
        outs=[shape((nodes, share)), shape((slots, share))],
        flops=2 * slots * nodes * share,
    )

    outgoing, summed = together((outgoing, summed))
    arrived = over_nodes(outgoing, blocks)
    sum_tiles = around(summed)
    twins = from_twin(near), from_twin(far)
    arrived, *sum_tiles = together((arrived, *sum_tiles))
    tiles = around(arrived)
    mixed_0, mixed_1, table = call(
        weights_first,
        me=who,
        near=[whole, near, twins[0], far, twins[1]],
        kept=[shape((3 * width, width))] * 2 + [shape((16, width), F32)],
        scratch=[pltpu.VMEM(whole.shape, BF16)],
    )
    (latent,) = call(
        node_first,
        me=who,
        far=[(latent, ()), (mixed_0, ()), (table, ())],
        near=sum_tiles,
        outs=[shape((nodes, width))],
        scratch=[pltpu.VMEM((nodes, width), BF16)],
        flops=3 * nodes * square,
    )
    held, sender_pre, oh_s, inc, oh_o = call(
        before_second,
        far=[
            (edge_w_in, (1, 0)),
            (edge_w_in, (1, 2)),
            (edge, ()),
            (senders, ()),
            (mixed_0, (pl.ds(0, 512), (512, width))),
            (table, ()),
            (edge_bias, ()),
        ],
        near=[latent, slot_row, receiver_row, link_rows],
        outs=[
            shape((edges, width), F32),
            shape((edges, width), F32),
            shape((edges, slots)),
            shape((nodes, edges)),
            shape((slots, nodes)),
        ],
        scratch=[pltpu.VMEM((edges, nodes), BF16)],
        flops=3 * edges * square,
    )
    (part,) = call(
        after_second,
        me=who,
        far=[
            (edge_w_in, (1, 1)),
            (edge_w_out, (1,)),
            *norms,
            (edge, ()),
            (senders, ()),
            (mixed_0, (pl.ds(512, 1024), (1024, width))),
            (table, ()),
        ],
        near=[held, sender_pre, oh_s, *tiles, inc],
        outs=[shape((nodes, width))],
        scratch=[pltpu.VMEM((edges, width), BF16)],
        flops=6 * edges * square,
    )
    parts = around(part)
    part, *grid_pieces = together((part, *grid_pieces))
    grid_tiles = handed(grid_pieces)
    (outgoing,) = call(
        node_second,
        me=who,
        far=[(mixed_1, ()), (table, ())],
        near=[latent, part, *parts[1:], oh_o],
        outs=[shape((slots, share))],
        scratch=[pltpu.VMEM((nodes, width), BF16)],
        flops=3 * nodes * square,
    )

    outgoing, whole_2, half_2 = together((outgoing, whole_2, half_2))
    arrived = over_nodes(outgoing, blocks)
    near, far = from_neighbours(whole_2, half_2)
    tiles = around(arrived)
    twins = from_twin(near), from_twin(far)
    (mixed_2,) = call(
        weights_last,
        me=who,
        near=[whole_2, near, twins[0], far, twins[1]],
        kept=[shape((3 * width, width))],
        scratch=[pltpu.VMEM(whole_2.shape, BF16)],
    )
    held, whole_cells, oh_m = call(
        before_links,
        me=who,
        far=[(edge_w_in, (2, 0)), (edge_w_in, (2, 2)), (edge_bias, ())],
        near=[m2g_edges, *grid_tiles, m2g_slots.reshape(1, links)],
        outs=[shape((links, width), F32), shape((cells, width)), shape((links, slots))],
        flops=2 * links * square,
    )
    pieces = call(
        after_links,
        me=who,
        far=[(edge_w_in, (2, 1)), (edge_w_out, (2,)), *norms, (mixed_2, ()), (table, ())],
        near=[held, oh_m, *tiles, m2g_edges, whole_cells],
        outs=[shape((cells, share))] * 4,
        scratch=[pltpu.VMEM((links, width), BF16), pltpu.VMEM((cells, width), BF16)],
        flops=8 * links * square,
    )
    pieces = handed(pieces)
    return call(join_body, me=who, near=pieces, outs=[shape((4 * cells, share))])[0]


def solution(mesh):
    in_specs = (
        P("node", "feat"),
        P(("node", "feat"), None),
        P("node", "feat"),
        P(("node", "feat"), None),
        P(("node", "feat")),
        P(("node", "feat")),
        P("node", None, None),
        P(("node", "feat")),
        P("node", None, None),
        P(),
        P(),
        P(),
        P(),
        P(),
        P(None, None, "feat", None),
        P(None, "feat", None),
        P(None, None, "feat"),
        P(None, "feat"),
        P(None, "feat"),
    )
    out_specs = P("node", "feat")

    return jax.shard_map(local, mesh=mesh, in_specs=in_specs, out_specs=out_specs, check_vma=False)
```

```python
import jax
import jax.numpy as jnp
from jax import lax
from jax.experimental import pallas as pl
from jax.experimental.pallas import tpu as pltpu
from jax.sharding import PartitionSpec as P


EPSILON = 1e-05
BF16 = jnp.bfloat16
F32 = jnp.float32

SMEM = pl.BlockSpec(memory_space=pltpu.SMEM)
VMEM = pl.BlockSpec(memory_space=pltpu.VMEM)
HBM = pl.BlockSpec(memory_space=pltpu.HBM)


class Fetched:
    def __init__(self, source, target, sem):
        self.copy = pltpu.make_async_copy(source, target, sem)
        self.copy.start()
        self.target = target

    def get(self):
        if self.copy is not None:
            self.copy.wait()
            self.copy = None
        return self.target


class Kept:
    def __init__(self, ref, target, sem):
        self.ref = ref
        self.copy = pltpu.make_async_copy(ref, target, sem)

    def put(self, value):
        self.ref[...] = value
        self.copy.start()


def block_of(ref, index):
    if not index:
        return ref
    return ref.at[tuple(i for i in index if not isinstance(i, tuple))]


def call(body, *, me=None, far=(), passed=(), near=(), kept=(), outs=(), scratch=(), flops=0):
    wanted = [*far, *passed]
    far_arrays = []
    for array, _ in wanted:
        if not any(array is other for other in far_arrays):
            far_arrays.append(array)
    places = [next(k for k, other in enumerate(far_arrays) if other is a) for a, _ in wanted]
    blocks = [
        tuple(array.shape[len(index) :]) if all(isinstance(i, int) for i in index) else index[-1]
        for array, index in wanted
    ]
    scalars = [] if me is None else [me]
    counts = [len(scalars), len(far_arrays), len(near), len(kept), len(outs), len(passed)]
    counts += [len(far), len(kept)]

    def kernel(*refs):
        groups, at = [], 0
        for count in counts:
            groups.append(refs[at : at + count])
            at += count
        who, sources, near_refs, kept_refs, out_refs, passed_refs, buffers, kept_buffers = groups
        *extra, sems = refs[at:]
        fetched = [
            Fetched(block_of(sources[place], index), buffer, sems.at[k])
            for k, (place, (_, index), buffer) in enumerate(
                zip(places, wanted, [*buffers, *passed_refs])
            )
        ]
        holders = [
            Kept(buffer, target, sems.at[len(wanted) + k])
            for k, (buffer, target) in enumerate(zip(kept_buffers, kept_refs))
        ]
        body(*who, *fetched, *near_refs, *holders, *out_refs, *extra)
        for item in fetched:
            item.get()
        for item in holders:
            item.copy.wait()

    moved = sum(a.size * a.dtype.itemsize for a in (*near, *kept, *outs))
    moved += sum(2 * 512 * 512 for _ in wanted)
    fixed = [pltpu.with_memory_space_constraint(array, pltpu.HBM) for array in far_arrays]
    return pl.pallas_call(
        kernel,
        out_shape=[pltpu.HBM(k.shape, k.dtype) for k in kept]
        + list(outs)
        + [pltpu.VMEM(b, a.dtype) for b, (a, _) in zip(blocks[len(far) :], passed)],
        in_specs=[SMEM] * len(scalars) + [HBM] * len(fixed) + [VMEM] * len(near),
        out_specs=[HBM] * len(kept) + [VMEM] * (len(outs) + len(passed)),
        scratch_shapes=[pltpu.VMEM(b, array.dtype) for b, (array, _) in zip(blocks, far)]
        + [pltpu.VMEM(k.shape, k.dtype) for k in kept]
        + list(scratch)
        + [pltpu.SemaphoreType.DMA((max(1, len(wanted) + len(kept)),))],
        compiler_params=pltpu.CompilerParams(vmem_limit_bytes=20 << 20),
        cost_estimate=pl.CostEstimate(flops=flops, bytes_accessed=moved, transcendentals=0),
    )(*scalars, *fixed, *near)


def shape(dims, dtype=BF16):
    return jax.ShapeDtypeStruct(dims, dtype)


def dot(a, b):
    return jnp.dot(a, b, preferred_element_type=F32)


def mask(condition):
    return jnp.where(condition, 1.0, 0.0).astype(BF16)


def column_one_hot(index_row, out):
    count = index_row.shape[1]
    turned = jnp.broadcast_to(index_row, (128, count)).T
    lane = lax.broadcasted_iota(jnp.int32, (count, 128), 1)
    for base in range(0, out.shape[1], 128):
        out[:, base : base + 128] = mask(turned == lane + base)


def table_one_hot(table, out):
    slot, blocks = table.shape
    lane = lax.broadcasted_iota(jnp.int32, (slot, out.shape[1]), 1)
    whole = table[...]
    for block in range(blocks):
        out[block * slot : (block + 1) * slot, :] = mask(whole[:, block : block + 1] == lane)


def row_one_hot(index_row, out):
    out[...] = mask(index_row == lax.broadcasted_iota(jnp.int32, out.shape, 0))


def owner(me, shift):
    return lax.rem(me[0] + (4 - shift), 4)


def lanes(index):
    return pl.ds(pl.multiple_of(index * 128, 128), 128)


def rows_at(index, height):
    return pl.ds(pl.multiple_of(index * height, height), height)


def silu(v):
    half = 0.5 * v
    return half + half * jnp.tanh(half)


def layer_norm(v, gain, shift):
    mean = jnp.mean(v, axis=-1, keepdims=True)
    variance = jnp.mean(v * v, axis=-1, keepdims=True) - mean * mean
    return (v - mean) * lax.rsqrt(variance + EPSILON) * gain + shift


def by_rows(count, size, step):
    def one(i, carry):
        step(pl.ds(pl.multiple_of(i * size, size), size))
        return carry

    lax.fori_loop(0, count // size, one, 0)


def first_gather(table, nodes, out, one_hot):
    table_one_hot(table.get(), one_hot)
    out[...] = dot(one_hot[...], nodes.get()[...]).astype(BF16)


def setup_kernel(me, w_in, w_out, bias, gain, shift, grid, *refs):
    outs, (first, last, cells, small, sems) = refs[:8], refs[8:]
    part = w_out.shape[1]
    pairs = [(grid, cells)]
    for k in range(3):
        target, base = (first, 3 * part * k) if k < 2 else (last, 0)
        for row in range(2):
            pairs.append((w_in.at[k, row], target.at[pl.ds(base + row * part, part)]))
        pairs.append((w_out.at[k], target.at[pl.ds(base + 2 * part, part)]))
    loads = [pltpu.make_async_copy(a, b, sems.at[n]) for n, (a, b) in enumerate(pairs)]
    for load in loads:
        load.start()
    small[...] = jnp.zeros_like(small)
    for k in range(3):
        small[2 * k : 2 * k + 2, :] = bias[k]
    small[6:9, :] = gain[...]
    small[9:12, :] = shift[...]
    rest = small[...]
    tail = 6 * part
    first[tail:, :] = jnp.zeros((first.shape[0] - tail, first.shape[1]), BF16)
    for plane in range(3):
        piece = rest.astype(BF16)
        first[tail : tail + 16, plane * part : (plane + 1) * part] = piece
        rest = rest - piece.astype(F32)
    for load in loads:
        load.wait()
    half, height = first.shape[0] // 2, cells.shape[0] // 4
    pairs = [(first, outs[0]), (first.at[rows_at(me[1], half)], outs[1])]
    pairs += [(last, outs[2]), (last.at[rows_at(me[1], last.shape[0] // 2)], outs[3])]
    for k in range(4):
        pairs.append((cells.at[rows_at(lax.rem(me[0] + k, 4), height)], outs[4 + k]))
    stores = [pltpu.make_async_copy(a, b, sems.at[n]) for n, (a, b) in enumerate(pairs)]
    for store in stores:
        store.start()
    for store in stores:
        store.wait()


def setup(who, w_in, w_out, bias, gain, shift, grid):
    share, width = w_out.shape[1:]
    first, last = 6 * share + 32, 3 * share
    heights = [first, first // 2, last, last // 2]
    return pl.pallas_call(
        setup_kernel,
        out_shape=[pltpu.HBM((h, width), BF16) for h in heights]
        + [pltpu.HBM((grid.shape[0] // 4, share), BF16)] * 4,
        in_specs=[SMEM, HBM, HBM, VMEM, VMEM, VMEM, HBM],
        out_specs=[HBM] * 8,
        scratch_shapes=[
            pltpu.VMEM((first, width), BF16),
            pltpu.VMEM((last, width), BF16),
            pltpu.VMEM(grid.shape, BF16),
            pltpu.VMEM((16, share), F32),
            pltpu.SemaphoreType.DMA((10,)),
        ],
        name="setup",
        compiler_params=pltpu.CompilerParams(vmem_limit_bytes=20 << 20),
        cost_estimate=pl.CostEstimate(flops=0, bytes_accessed=4 << 20, transcendentals=0),
    )(
        who,
        pltpu.with_memory_space_constraint(w_in, pltpu.HBM),
        pltpu.with_memory_space_constraint(w_out, pltpu.HBM),
        bias,
        gain,
        shift,
        pltpu.with_memory_space_constraint(grid, pltpu.HBM),
    )


def placed(me, tiles, far, outs):
    mine, near, other, half, other_half = tiles
    height, first = half.shape[0], 1 + 2 * me[1]
    far[rows_at(me[1], height), :] = half[...]
    far[rows_at(1 - me[1], height), :] = other_half[...]
    owned = [(mine, 0), (near, first), (other, 4 - first), (far, 2)]
    owned = [(tile, lax.rem(me[0] + (4 - shift), 4)) for tile, shift in owned]
    for tile, base in owned:
        for layer, out in enumerate(outs):
            for part in range(3):
                row = (3 * layer + part) * 128
                out[pl.ds(pl.multiple_of(part * 512 + base * 128, 128), 128), :] = tile[
                    row : row + 128, :
                ]
    return owned


def weights_first(me, mine, near, other, half, other_half, kept, one, two, table, far):
    owned = placed(me, (mine, near, other, half, other_half), far, (one, two))
    for tile, base in owned:
        planes = [tile[768:784, k * 128 : (k + 1) * 128].astype(F32) for k in range(3)]
        table[:, lanes(base)] = planes[0] + planes[1] + planes[2]
    kept.put(table[...])


def weights_last(me, mine, near, other, half, other_half, out, far):
    placed(me, (mine, near, other, half, other_half), far, (out.ref,))
    out.copy.start()


def before_first(
    me,
    w_e,
    w_r,
    bias,
    w_s,
    w_o,
    edge,
    n0,
    n1,
    n2,
    n3,
    slots,
    receivers,
    rows,
    nodes,
    out,
    oh_s,
    inc,
    oh_o,
    oh_r,
):
    for k, tile in enumerate((n0, n1, n2, n3)):
        nodes.ref[:, lanes(owner(me, k))] = tile[...]
    nodes.copy.start()
    column_one_hot(receivers[...], oh_r)
    column_one_hot(slots[...], oh_s)
    row_one_hot(receivers[...], inc)
    table_one_hot(rows, oh_o)
    edges, we, wr, first = edge.get(), w_e.get(), w_r.get(), bias.get()

    def step(at):
        taken = dot(oh_r[at, :], nodes.ref[...]).astype(BF16)
        out[at, :] = dot(edges[at, :], we[...]) + dot(taken, wr[...]) + first[0, 0:1, :]

    by_rows(out.shape[0], 128, step)


def before_second(
    w_e,
    w_r,
    bias,
    w_s,
    w_o,
    edge,
    senders,
    nodes,
    mixed,
    table,
    slots,
    receivers,
    rows,
    out,
    sender_pre,
    oh_s,
    inc,
    oh_o,
    oh_r,
):
    column_one_hot(receivers[...], oh_r)
    column_one_hot(slots[...], oh_s)
    row_one_hot(receivers[...], inc)
    table_one_hot(rows, oh_o)
    edges, old, we, wr, first = edge.get(), senders.get(), w_e.get(), w_r.get(), bias.get()

    def step(at):
        taken = dot(oh_r[at, :], nodes[...]).astype(BF16)
        out[at, :] = dot(edges[at, :], we[...]) + dot(taken, wr[...]) + first[1, 0:1, :]
        sender_pre[at, :] = table[0:1, :] + dot(old[at, :], mixed[0:512, :])

    by_rows(out.shape[0], 256, step)


def before_links(me, w_e, w_r, bias, edge, g0, g1, g2, g3, slots, out, cells, oh_m, spread):
    for k, tile in enumerate((g0, g1, g2, g3)):
        cells.ref[:, lanes(owner(me, k))] = tile[...]
    cells.copy.start()
    links, count = out.ref.shape[0], cells.ref.shape[0]
    row = lax.broadcasted_iota(jnp.int32, (links, count), 0)
    first = 3 * lax.broadcasted_iota(jnp.int32, (links, count), 1)
    spread[...] = mask((row >= first) & (row < first + 3))
    column_one_hot(slots[...], oh_m.ref)
    oh_m.copy.start()
    edges, we, wr, start = edge.get(), w_e.get(), w_r.get(), bias.get()

    def step(at):
        taken = dot(spread[at, :], cells.ref[...]).astype(BF16)
        out.ref[at, :] = dot(edges[at, :], we[...]) + dot(taken, wr[...]) + start[2, 0:1, :]

    by_rows(links, 128, step)
    out.copy.start()


def join_tiles(me, tiles, joined):
    for k, tile in enumerate(tiles):
        joined[:, lanes(owner(me, k))] = tile[...]


def edge_tail(layer, before, senders, w_s, w_o, norms, edge):
    bias, gain, shift = norms
    hidden = silu(before + dot(senders, w_s[...])).astype(BF16)
    projected = dot(hidden, w_o[...]) + bias[layer, 1:2, :]
    scale, offset = gain[layer : layer + 1, :], shift[layer : layer + 1, :]
    return (edge.astype(F32) + layer_norm(projected, scale, offset)).astype(BF16)


def node_tail(layer, latent, pre, summed, mixed, table):
    hidden = silu(pre + dot(summed, mixed[512:1024, :])).astype(BF16)
    projected = dot(hidden, mixed[1024:1536, :]) + table[2 * layer + 1 : 2 * layer + 2, :]
    normed = layer_norm(
        projected, table[6 + layer : 7 + layer, :], table[9 + layer : 10 + layer, :]
    )
    return (latent.astype(F32) + normed).astype(BF16)


def after_first(
    me,
    bias,
    gain,
    shift,
    before,
    one_hot,
    w_s,
    w_o,
    edge,
    a0,
    a1,
    a2,
    a3,
    inc,
    new,
    senders,
    p0,
    p1,
    p2,
    p3,
    joined,
    held,
):
    join_tiles(me, (a0, a1, a2, a3), joined)
    norms = bias.get(), gain.get(), shift.get()

    def step(at):
        taken = dot(one_hot[at, :], joined[...]).astype(BF16)
        senders.ref[at, :] = taken
        new.ref[at, :] = edge_tail(0, before[at, :], taken, w_s, w_o, norms, edge[at, :])

    by_rows(edge.shape[0], 256, step)
    senders.copy.start()
    new.copy.start()
    held[...] = dot(inc[...], new.ref[...]).astype(BF16)
    for k, out in enumerate((p0, p1, p2, p3)):
        out[...] = held[:, lanes(lax.rem(me[0] + k, 4))]


def after_second(
    me,
    bias,
    gain,
    shift,
    before,
    sender_pre,
    one_hot,
    w_s,
    w_o,
    edge,
    senders,
    mixed,
    table,
    a0,
    a1,
    a2,
    a3,
    inc,
    part,
    joined,
    new,
):
    join_tiles(me, (a0, a1, a2, a3), joined)
    norms = bias.get(), gain.get(), shift.get()

    def step(at):
        summed = dot(one_hot[at, :], joined[...]).astype(BF16)
        latest = node_tail(0, senders[at, :], sender_pre[at, :], summed, mixed, table)
        new[at, :] = edge_tail(1, before[at, :], latest, w_s, w_o, norms, edge[at, :])

    by_rows(new.shape[0], 256, step)
    part[...] = dot(inc[...], new[...]).astype(BF16)


def after_links(
    me,
    one_hot,
    w_s,
    before,
    w_o,
    bias,
    gain,
    shift,
    edge,
    mixed,
    table,
    cells,
    joined,
    o0,
    o1,
    o2,
    o3,
    new,
    held,
):
    spread, first, second, start, old = (x.get() for x in (one_hot, w_s, w_o, before, edge))
    norms = bias.get(), gain.get(), shift.get()

    def step(at):
        senders = dot(spread[at, :], joined[...]).astype(BF16)
        new[at, :] = edge_tail(2, start[at, :], senders, first, second, norms, old[at, :])

    by_rows(new.shape[0], 192, step)
    links, count = new.shape[0], held.shape[0]
    low = 3 * lax.broadcasted_iota(jnp.int32, (count, links), 0)
    column = lax.broadcasted_iota(jnp.int32, (count, links), 1)
    added = dot(mask((column >= low) & (column < low + 3)), new[...]).astype(BF16)
    rows, weights, latent = table.get(), mixed.get(), cells.get()[...]
    pre = rows[4:5, :] + dot(latent, weights[0:512, :])
    held[...] = node_tail(2, latent, pre, added, weights, rows)
    for k, out in enumerate((o0, o1, o2, o3)):
        out[...] = held[:, lanes(lax.rem(me[0] + k, 4))]


def sum_body(s0, s1, s2, s3, one_hot, summed, outgoing):
    total = s0[...].astype(F32) + s1[...].astype(F32) + s2[...].astype(F32) + s3[...].astype(F32)
    summed[...] = total.astype(BF16)
    outgoing[...] = dot(one_hot[...], summed[...]).astype(BF16)


def node_first(me, latent, mixed, table, s0, s1, s2, s3, new, summed):
    for k, tile in enumerate((s0, s1, s2, s3)):
        summed[:, lanes(owner(me, k))] = tile[...]
    old = latent.get()

    def step(at):
        pre = table[0:1, :] + dot(old[at, :], mixed[0:512, :])
        new[at, :] = node_tail(0, old[at, :], pre, summed[at, :], mixed, table)

    by_rows(new.shape[0], 128, step)


def node_second(latent, mixed, table, p0, p1, p2, p3, one_hot, outgoing, new):
    total = p0[...].astype(F32) + p1[...].astype(F32) + p2[...].astype(F32) + p3[...].astype(F32)
    old = latent[...]
    pre = table[2:3, :] + dot(old, mixed[0:512, :])
    new[...] = node_tail(1, old, pre, total.astype(BF16), mixed, table)
    outgoing[...] = dot(one_hot[...], new[...]).astype(BF16)


def join_body(me, r0, r1, r2, r3, out):
    for k, tile in enumerate((r0, r1, r2, r3)):
        out[rows_at(owner(me, k), 128), :] = tile[...]


def moved(x, shift):
    return lax.ppermute(x, "feat", [(i, (i + shift) % 4) for i in range(4)])


def around(x):
    three, two, one = (moved(x, k) for k in (3, 2, 1))
    return [x, one, two, three]


def handed(pieces):
    three, two, one = (moved(pieces[k], k) for k in (3, 2, 1))
    return [pieces[0], one, two, three]


def from_neighbours(whole, half):
    size = lax.axis_size("node")
    ring = [
        (n * 4 + f, n * 4 + (f + (1 if n % 2 == 0 else 3)) % 4) for n in range(size) for f in range(4)
    ]
    return lax.ppermute(whole, ("node", "feat"), ring), moved(half, 2)


def from_twin(x):
    return lax.ppermute(x, "node", [(n, n ^ 1) for n in range(lax.axis_size("node"))])


def over_nodes(x, blocks):
    tiles = x.reshape(blocks, x.shape[0] // blocks, x.shape[1])
    return lax.all_to_all(tiles, "node", split_axis=0, concat_axis=0, tiled=True).reshape(x.shape)


together = lax.optimization_barrier


def local(
    mesh_nodes,
    mesh_edges,
    grid_nodes,
    m2g_edges,
    edge_receivers,
    edge_slots,
    send_rows,
    m2g_slots,
    m2g_send_rows,
    edge_w_in,
    edge_w_out,
    edge_bias,
    edge_gain,
    edge_shift,
    node_w_in,
    node_w_out,
    node_bias,
    node_gain,
    node_shift,
):
    who = jnp.stack([lax.axis_index("feat"), lax.rem(lax.axis_index("node"), 2)]).astype(jnp.int32)
    nodes, share = mesh_nodes.shape
    edges, width = mesh_edges.shape
    links = m2g_edges.shape[0]
    blocks, slot = send_rows.shape[1:]
    slots = blocks * slot
    cells = grid_nodes.shape[0] // 4
    square = 2 * width * width
    rows, link_rows = send_rows[0].T, m2g_send_rows[0].T
    norms = [(edge_bias, ()), (edge_gain, ()), (edge_shift, ())]
    slot_row, receiver_row = edge_slots.reshape(1, edges), edge_receivers.reshape(1, edges)

    (outgoing,) = call(
        first_gather,
        far=[(rows, ()), (mesh_nodes, ())],
        outs=[shape((slots, share))],
        scratch=[pltpu.VMEM((slots, nodes), BF16)],
    )
    outgoing, late_nodes, late_who = together((outgoing, mesh_nodes, who))
    arrived = over_nodes(outgoing, blocks)
    node_tiles = around(late_nodes)
    prepared = setup(late_who, node_w_in, node_w_out, node_bias, node_gain, node_shift, grid_nodes)
    whole, half, whole_2, half_2, *grid_pieces = prepared
    arrived, half = together((arrived, half))
    tiles = around(arrived)
    latent, held, oh_s, inc, oh_o, w_s, w_o, edge = call(
        before_first,
        me=who,
        far=[(edge_w_in, (0, 0)), (edge_w_in, (0, 2)), (edge_bias, ())],
        passed=[(edge_w_in, (0, 1)), (edge_w_out, (0,)), (mesh_edges, ())],
        near=[*node_tiles, slot_row, receiver_row, rows],
        kept=[shape((nodes, width))],
        outs=[
            shape((edges, width), F32),
            shape((edges, slots)),
            shape((nodes, edges)),
            shape((slots, nodes)),
        ],
        scratch=[pltpu.VMEM((edges, nodes), BF16)],
        flops=2 * edges * square,
    )
    edge, senders, *partial = call(
        after_first,
        me=who,
        far=norms,
        near=[held, oh_s, w_s, w_o, edge, *tiles, inc],
        kept=[shape((edges, width)), shape((edges, width))],
        outs=[shape((nodes, share))] * 4,
        scratch=[pltpu.VMEM((slots, width), BF16), pltpu.VMEM((nodes, width), BF16)],
        flops=4 * edges * square,
    )
    *partial, whole, half = together((*partial, whole, half))
    sums = handed(partial)
    near, far = from_neighbours(whole, half)
    summed, outgoing = call(
        sum_body,
        near=[*sums, oh_o],
        outs=[shape((nodes, share)), shape((slots, share))],
        flops=2 * slots * nodes * share,
    )

    outgoing, summed = together((outgoing, summed))
    arrived = over_nodes(outgoing, blocks)
    sum_tiles = around(summed)
    twins = from_twin(near), from_twin(far)
    tiles = around(arrived)
    far_table, mixed_0, mixed_1, table = call(
        weights_first,
        me=who,
        near=[whole, near, twins[0], far, twins[1]],
        kept=[shape((16, width), F32)],
        outs=[shape((3 * width, width))] * 2 + [shape((16, width), F32)],
        scratch=[pltpu.VMEM(whole.shape, BF16)],
    )
    (latent,) = call(
        node_first,
        me=who,
        far=[(latent, ())],
        near=[mixed_0, table, *sum_tiles],
        outs=[shape((nodes, width))],
        scratch=[pltpu.VMEM((nodes, width), BF16)],
        flops=3 * nodes * square,
    )
    held, sender_pre, oh_s, inc, oh_o, w_s, w_o, edge, senders = call(
        before_second,
        far=[(edge_w_in, (1, 0)), (edge_w_in, (1, 2)), (edge_bias, ())],
        passed=[(edge_w_in, (1, 1)), (edge_w_out, (1,)), (edge, ()), (senders, ())],
        near=[latent, mixed_0, table, slot_row, receiver_row, link_rows],
        outs=[
            shape((edges, width), F32),
            shape((edges, width), F32),
            shape((edges, slots)),
            shape((nodes, edges)),
            shape((slots, nodes)),
        ],
        scratch=[pltpu.VMEM((edges, nodes), BF16)],
        flops=3 * edges * square,
    )
    (part,) = call(
        after_second,
        me=who,
        far=norms,
        near=[held, sender_pre, oh_s, w_s, w_o, edge, senders, mixed_0, table, *tiles, inc],
        outs=[shape((nodes, width))],
        scratch=[pltpu.VMEM((slots, width), BF16), pltpu.VMEM((edges, width), BF16)],
        flops=6 * edges * square,
    )
    parts = around(part)
    (outgoing,) = call(
        node_second,
        near=[latent, mixed_1, table, *parts, oh_o],
        outs=[shape((slots, width))],
        scratch=[pltpu.VMEM((nodes, width), BF16)],
        flops=3 * nodes * square,
    )

    outgoing, whole_2, half_2, *grid_pieces = together((outgoing, whole_2, half_2, *grid_pieces))
    arrived = over_nodes(outgoing, blocks)
    near, far = from_neighbours(whole_2, half_2)
    grid_tiles = handed(grid_pieces)
    twins = from_twin(near), from_twin(far)
    (mixed_2,) = call(
        weights_last,
        me=who,
        near=[whole_2, near, twins[0], far, twins[1]],
        kept=[shape((3 * width, width))],
        scratch=[pltpu.VMEM(whole_2.shape, BF16)],
    )
    held, whole_cells, oh_m = call(
        before_links,
        me=who,
        far=[
            (edge_w_in, (2, 0)),
            (edge_w_in, (2, 2)),
            (edge_bias, ()),
            (m2g_edges, ()),
        ],
        near=[*grid_tiles, m2g_slots.reshape(1, links)],
        kept=[shape((links, width), F32), shape((cells, width)), shape((links, slots))],
        scratch=[pltpu.VMEM((links, cells), BF16)],
        flops=2 * links * square,
    )
    arrived, held, mixed_2 = together((arrived, held, mixed_2))
    pieces = call(
        after_links,
        me=who,
        far=[
            (oh_m, ()),
            (edge_w_in, (2, 1)),
            (held, ()),
            (edge_w_out, (2,)),
            *norms,
            (m2g_edges, ()),
            (mixed_2, ()),
            (far_table, ()),
            (whole_cells, ()),
        ],
        near=[arrived],
        outs=[shape((cells, share))] * 4,
        scratch=[pltpu.VMEM((links, width), BF16), pltpu.VMEM((cells, width), BF16)],
        flops=8 * links * square,
    )
    pieces = handed(pieces)
    return call(join_body, me=who, near=pieces, outs=[shape((4 * cells, share))])[0]


def solution(mesh):
    in_specs = (
        P("node", "feat"),
        P(("node", "feat"), None),
        P("node", "feat"),
        P(("node", "feat"), None),
        P(("node", "feat")),
        P(("node", "feat")),
        P("node", None, None),
        P(("node", "feat")),
        P("node", None, None),
        P(),
        P(),
        P(),
        P(),
        P(),
        P(None, None, "feat", None),
        P(None, "feat", None),
        P(None, None, "feat"),
        P(None, "feat"),
        P(None, "feat"),
    )
    out_specs = P("node", "feat")

    return jax.shard_map(local, mesh=mesh, in_specs=in_specs, out_specs=out_specs, check_vma=False)
```

```python
import jax
import jax.numpy as jnp
from jax import lax
from jax.experimental import pallas as pl
from jax.experimental.pallas import tpu as pltpu
from jax.sharding import PartitionSpec as P


EPSILON = 1e-05
BF16 = jnp.bfloat16
F32 = jnp.float32

SMEM = pl.BlockSpec(memory_space=pltpu.SMEM)
VMEM = pl.BlockSpec(memory_space=pltpu.VMEM)
HBM = pl.BlockSpec(memory_space=pltpu.HBM)


class Fetched:
    def __init__(self, source, target, sem):
        self.copy = pltpu.make_async_copy(source, target, sem)
        self.copy.start()
        self.target = target

    def get(self):
        if self.copy is not None:
            self.copy.wait()
            self.copy = None
        return self.target


class Kept:
    def __init__(self, ref, target, sem):
        self.ref, self.target, self.sem = ref, target, sem
        self.copy = pltpu.make_async_copy(ref, target, sem)

    def send(self, at):
        pltpu.make_async_copy(self.ref.at[at], self.target.at[at], self.sem).start()

    def put(self, value):
        self.ref[...] = value
        self.copy.start()


def block_of(ref, index):
    if not index:
        return ref
    return ref.at[tuple(i for i in index if not isinstance(i, tuple))]


def call(body, *, me=None, far=(), passed=(), near=(), kept=(), outs=(), scratch=(), flops=0):
    wanted = [*far, *passed]
    far_arrays = []
    for array, _ in wanted:
        if not any(array is other for other in far_arrays):
            far_arrays.append(array)
    places = [next(k for k, other in enumerate(far_arrays) if other is a) for a, _ in wanted]
    blocks = [
        tuple(array.shape[len(index) :]) if all(isinstance(i, int) for i in index) else index[-1]
        for array, index in wanted
    ]
    scalars = [] if me is None else [me]
    counts = [len(scalars), len(far_arrays), len(near), len(kept), len(outs), len(passed)]
    counts += [len(far), len(kept)]

    def kernel(*refs):
        groups, at = [], 0
        for count in counts:
            groups.append(refs[at : at + count])
            at += count
        who, sources, near_refs, kept_refs, out_refs, passed_refs, buffers, kept_buffers = groups
        *extra, sems = refs[at:]
        fetched = [
            Fetched(block_of(sources[place], index), buffer, sems.at[k])
            for k, (place, (_, index), buffer) in enumerate(
                zip(places, wanted, [*buffers, *passed_refs])
            )
        ]
        holders = [
            Kept(buffer, target, sems.at[len(wanted) + k])
            for k, (buffer, target) in enumerate(zip(kept_buffers, kept_refs))
        ]
        body(*who, *fetched, *near_refs, *holders, *out_refs, *extra)
        for item in fetched:
            item.get()
        for item in holders:
            item.copy.wait()

    moved = sum(a.size * a.dtype.itemsize for a in (*near, *kept, *outs))
    moved += sum(2 * 512 * 512 for _ in wanted)
    fixed = [pltpu.with_memory_space_constraint(array, pltpu.HBM) for array in far_arrays]
    return pl.pallas_call(
        kernel,
        out_shape=[pltpu.HBM(k.shape, k.dtype) for k in kept]
        + list(outs)
        + [pltpu.VMEM(b, a.dtype) for b, (a, _) in zip(blocks[len(far) :], passed)],
        in_specs=[SMEM] * len(scalars) + [HBM] * len(fixed) + [VMEM] * len(near),
        out_specs=[HBM] * len(kept) + [VMEM] * (len(outs) + len(passed)),
        scratch_shapes=[pltpu.VMEM(b, array.dtype) for b, (array, _) in zip(blocks, far)]
        + [pltpu.VMEM(k.shape, k.dtype) for k in kept]
        + list(scratch)
        + [pltpu.SemaphoreType.DMA((max(1, len(wanted) + len(kept)),))],
        compiler_params=pltpu.CompilerParams(vmem_limit_bytes=20 << 20),
        cost_estimate=pl.CostEstimate(flops=flops, bytes_accessed=moved, transcendentals=0),
    )(*scalars, *fixed, *near)


def shape(dims, dtype=BF16):
    return jax.ShapeDtypeStruct(dims, dtype)


def dot(a, b):
    return jnp.dot(a, b, preferred_element_type=F32)


def mask(condition):
    return jnp.where(condition, 1.0, 0.0).astype(BF16)


def column_one_hot(index_row, out):
    count = index_row.shape[1]
    turned = jnp.broadcast_to(index_row, (128, count)).T
    lane = lax.broadcasted_iota(jnp.int32, (count, 128), 1)
    for base in range(0, out.shape[1], 128):
        out[:, base : base + 128] = mask(turned == lane + base)


def table_one_hot(table, out):
    slot, blocks = table.shape
    lane = lax.broadcasted_iota(jnp.int32, (slot, out.shape[1]), 1)
    whole = table[...]
    for block in range(blocks):
        out[block * slot : (block + 1) * slot, :] = mask(whole[:, block : block + 1] == lane)


def row_one_hot(index_row, out):
    out[...] = mask(index_row == lax.broadcasted_iota(jnp.int32, out.shape, 0))


def owner(me, shift):
    return lax.rem(me[0] + (4 - shift), 4)


def lanes(index):
    return pl.ds(pl.multiple_of(index * 128, 128), 128)


def rows_at(index, height):
    return pl.ds(pl.multiple_of(index * height, height), height)


def silu(v):
    half = 0.5 * v
    return half + half * jnp.tanh(half)


def layer_norm(v, gain, shift):
    mean = jnp.mean(v, axis=-1, keepdims=True)
    variance = jnp.mean(v * v, axis=-1, keepdims=True) - mean * mean
    return (v - mean) * lax.rsqrt(variance + EPSILON) * gain + shift


def by_rows(count, size, step):
    def one(i, carry):
        step(pl.ds(pl.multiple_of(i * size, size), size))
        return carry

    lax.fori_loop(0, count // size, one, 0)


def first_gather(table, nodes, out, one_hot):
    table_one_hot(table.get(), one_hot)
    out[...] = dot(one_hot[...], nodes.get()[...]).astype(BF16)


def setup_kernel(me, w_in, w_out, bias, gain, shift, grid, *refs):
    outs, (first, last, cells, small, sems) = refs[:8], refs[8:]
    part = w_out.shape[1]
    pairs = [(grid, cells)]
    for k in range(3):
        target, base = (first, 3 * part * k) if k < 2 else (last, 0)
        for row in range(2):
            pairs.append((w_in.at[k, row], target.at[pl.ds(base + row * part, part)]))
        pairs.append((w_out.at[k], target.at[pl.ds(base + 2 * part, part)]))
    loads = [pltpu.make_async_copy(a, b, sems.at[n]) for n, (a, b) in enumerate(pairs)]
    for load in loads:
        load.start()
    small[...] = jnp.zeros_like(small)
    for k in range(3):
        small[2 * k : 2 * k + 2, :] = bias[k]
    small[6:9, :] = gain[...]
    small[9:12, :] = shift[...]
    rest = small[...]
    tail = 6 * part
    first[tail:, :] = jnp.zeros((first.shape[0] - tail, first.shape[1]), BF16)
    for plane in range(3):
        piece = rest.astype(BF16)
        first[tail : tail + 16, plane * part : (plane + 1) * part] = piece
        rest = rest - piece.astype(F32)
    for load in loads:
        load.wait()
    half, height = first.shape[0] // 2, cells.shape[0] // 4
    pairs = [(first, outs[0]), (first.at[rows_at(me[1], half)], outs[1])]
    pairs += [(last, outs[2]), (last.at[rows_at(me[1], last.shape[0] // 2)], outs[3])]
    for k in range(4):
        pairs.append((cells.at[rows_at(lax.rem(me[0] + k, 4), height)], outs[4 + k]))
    stores = [pltpu.make_async_copy(a, b, sems.at[n]) for n, (a, b) in enumerate(pairs)]
    for store in stores:
        store.start()
    for store in stores:
        store.wait()


def setup(who, w_in, w_out, bias, gain, shift, grid):
    share, width = w_out.shape[1:]
    first, last = 6 * share + 32, 3 * share
    heights = [first, first // 2, last, last // 2]
    return pl.pallas_call(
        setup_kernel,
        out_shape=[pltpu.HBM((h, width), BF16) for h in heights]
        + [pltpu.HBM((grid.shape[0] // 4, share), BF16)] * 4,
        in_specs=[SMEM, HBM, HBM, VMEM, VMEM, VMEM, HBM],
        out_specs=[HBM] * 8,
        scratch_shapes=[
            pltpu.VMEM((first, width), BF16),
            pltpu.VMEM((last, width), BF16),
            pltpu.VMEM(grid.shape, BF16),
            pltpu.VMEM((16, share), F32),
            pltpu.SemaphoreType.DMA((10,)),
        ],
        name="setup",
        compiler_params=pltpu.CompilerParams(vmem_limit_bytes=20 << 20),
        cost_estimate=pl.CostEstimate(flops=0, bytes_accessed=4 << 20, transcendentals=0),
    )(
        who,
        pltpu.with_memory_space_constraint(w_in, pltpu.HBM),
        pltpu.with_memory_space_constraint(w_out, pltpu.HBM),
        bias,
        gain,
        shift,
        pltpu.with_memory_space_constraint(grid, pltpu.HBM),
    )


def placed(me, tiles, far, outs):
    mine, near, other, half, other_half = tiles
    height, first = half.shape[0], 1 + 2 * me[1]
    far[rows_at(me[1], height), :] = half[...]
    far[rows_at(1 - me[1], height), :] = other_half[...]
    owned = [(mine, 0), (near, first), (other, 4 - first), (far, 2)]
    owned = [(tile, lax.rem(me[0] + (4 - shift), 4)) for tile, shift in owned]
    for tile, base in owned:
        for layer, out in enumerate(outs):
            for part in range(3):
                row = (3 * layer + part) * 128
                out[pl.ds(pl.multiple_of(part * 512 + base * 128, 128), 128), :] = tile[
                    row : row + 128, :
                ]
    return owned


def weights_first(me, mine, near, other, half, other_half, kept, one, two, table, far):
    owned = placed(me, (mine, near, other, half, other_half), far, (one, two))
    for tile, base in owned:
        planes = [tile[768:784, k * 128 : (k + 1) * 128].astype(F32) for k in range(3)]
        table[:, lanes(base)] = planes[0] + planes[1] + planes[2]
    kept.put(table[...])


def weights_last(me, mine, near, other, half, other_half, out, far):
    placed(me, (mine, near, other, half, other_half), far, (out.ref,))
    out.copy.start()


def before_first(
    me,
    w_e,
    w_r,
    bias,
    w_s,
    w_o,
    edge,
    n0,
    n1,
    n2,
    n3,
    slots,
    receivers,
    rows,
    nodes,
    out,
    oh_s,
    inc,
    oh_o,
    oh_r,
):
    for k, tile in enumerate((n0, n1, n2, n3)):
        nodes.ref[:, lanes(owner(me, k))] = tile[...]
    nodes.copy.start()
    column_one_hot(receivers[...], oh_r)
    column_one_hot(slots[...], oh_s)
    row_one_hot(receivers[...], inc)
    table_one_hot(rows, oh_o)
    edges, we, wr, first = edge.get(), w_e.get(), w_r.get(), bias.get()

    def step(at):
        taken = dot(oh_r[at, :], nodes.ref[...]).astype(BF16)
        out[at, :] = dot(edges[at, :], we[...]) + dot(taken, wr[...]) + first[0, 0:1, :]

    by_rows(out.shape[0], 128, step)


def before_second(
    w_e,
    w_r,
    bias,
    w_s,
    w_o,
    edge,
    senders,
    nodes,
    mixed,
    table,
    slots,
    receivers,
    rows,
    out,
    sender_pre,
    oh_s,
    inc,
    oh_o,
    oh_r,
):
    column_one_hot(receivers[...], oh_r)
    column_one_hot(slots[...], oh_s)
    row_one_hot(receivers[...], inc)
    table_one_hot(rows, oh_o)
    edges, old, we, wr, first = edge.get(), senders.get(), w_e.get(), w_r.get(), bias.get()

    def step(at):
        taken = dot(oh_r[at, :], nodes[...]).astype(BF16)
        out[at, :] = dot(edges[at, :], we[...]) + dot(taken, wr[...]) + first[1, 0:1, :]
        sender_pre[at, :] = table[0:1, :] + dot(old[at, :], mixed[0:512, :])

    by_rows(out.shape[0], 256, step)


def before_links(me, w_e, w_r, bias, edge, g0, g1, g2, g3, slots, out, cells, oh_m, spread):
    for k, tile in enumerate((g0, g1, g2, g3)):
        cells.ref[:, lanes(owner(me, k))] = tile[...]
    cells.copy.start()
    links, count = out.ref.shape[0], cells.ref.shape[0]
    row = lax.broadcasted_iota(jnp.int32, (links, count), 0)
    first = 3 * lax.broadcasted_iota(jnp.int32, (links, count), 1)
    spread[...] = mask((row >= first) & (row < first + 3))
    column_one_hot(slots[...], oh_m.ref)
    oh_m.copy.start()
    edges, we, wr, start = edge.get(), w_e.get(), w_r.get(), bias.get()

    def step(at):
        taken = dot(spread[at, :], cells.ref[...]).astype(BF16)
        out.ref[at, :] = dot(edges[at, :], we[...]) + dot(taken, wr[...]) + start[2, 0:1, :]

    by_rows(links, 128, step)
    out.copy.start()


def pair_up(me, shifts, tiles, weights, base, joined, rows):
    for k, (shift, tile) in enumerate(zip(shifts, tiles)):
        joined[:, k * 128 : (k + 1) * 128] = tile[...]
        low = pl.multiple_of(base + owner(me, shift) * 128, 128)
        rows[k * 128 : (k + 1) * 128, :] = weights[pl.ds(low, 128), :]


def early_first(me, before, one_hot, w_s, own, two, total, part, joined, rows):
    pair_up(me, (0, 2), (own, two), w_s, 0, joined, rows)

    def step(at):
        part[at, :] = dot(one_hot[at, :], joined[...]).astype(BF16)
        total[at, :] = before[at, :] + dot(part[at, :], rows[...])

    by_rows(total.shape[0], 128, step)


def early_second(me, before, one_hot, mixed, own, two, total, joined, rows):
    pair_up(me, (0, 2), (own, two), mixed, 512, joined, rows)

    def step(at):
        part = dot(one_hot[at, :], joined[...]).astype(BF16)
        total[at, :] = before[at, :] + dot(part, rows[...])

    by_rows(total.shape[0], 128, step)


def edge_tail(layer, before, senders, w_s, w_o, norms, edge):
    return edge_close(layer, before + dot(senders, w_s[...]), w_o, norms, edge)


def edge_close(layer, pre, w_o, norms, edge):
    bias, gain, shift = norms
    hidden = silu(pre).astype(BF16)
    projected = dot(hidden, w_o[...]) + bias[layer, 1:2, :]
    scale, offset = gain[layer : layer + 1, :], shift[layer : layer + 1, :]
    return (edge.astype(F32) + layer_norm(projected, scale, offset)).astype(BF16)


def node_tail(layer, latent, pre, summed, mixed, table):
    return node_close(layer, latent, pre + dot(summed, mixed[512:1024, :]), mixed, table)


def node_close(layer, latent, pre, mixed, table):
    hidden = silu(pre).astype(BF16)
    projected = dot(hidden, mixed[1024:1536, :]) + table[2 * layer + 1 : 2 * layer + 2, :]
    normed = layer_norm(
        projected, table[6 + layer : 7 + layer, :], table[9 + layer : 10 + layer, :]
    )
    return (latent.astype(F32) + normed).astype(BF16)


def after_first(
    me,
    bias,
    gain,
    shift,
    total,
    early,
    one_hot,
    w_s,
    w_o,
    edge,
    a1,
    a3,
    inc,
    new,
    senders,
    p0,
    p1,
    p2,
    p3,
    joined,
    rows,
    held,
):
    pair_up(me, (1, 3), (a1, a3), w_s, 0, joined, rows)
    for k, shift_by in enumerate((0, 2)):
        senders.ref[:, lanes(owner(me, shift_by))] = early[:, k * 128 : (k + 1) * 128]
    norms = bias.get(), gain.get(), shift.get()
    for low in range(0, edge.shape[0], 256):
        at = pl.ds(low, 256)
        late = dot(one_hot[at, :], joined[...]).astype(BF16)
        for k, shift_by in enumerate((1, 3)):
            senders.ref[at, lanes(owner(me, shift_by))] = late[:, k * 128 : (k + 1) * 128]
        senders.send(at)
        new.ref[at, :] = edge_close(0, total[at, :] + dot(late, rows[...]), w_o, norms, edge[at, :])
        new.send(at)
    held[...] = dot(inc[...], new.ref[...]).astype(BF16)
    for k, out in enumerate((p0, p1, p2, p3)):
        out[...] = held[:, lanes(lax.rem(me[0] + k, 4))]


def after_second(
    me,
    bias,
    gain,
    shift,
    before,
    total,
    one_hot,
    w_s,
    w_o,
    edge,
    senders,
    mixed,
    table,
    a1,
    a3,
    inc,
    part,
    joined,
    rows,
    new,
):
    pair_up(me, (1, 3), (a1, a3), mixed, 512, joined, rows)
    norms = bias.get(), gain.get(), shift.get()

    def step(at):
        late = dot(one_hot[at, :], joined[...]).astype(BF16)
        pre = total[at, :] + dot(late, rows[...])
        latest = node_close(0, senders[at, :], pre, mixed, table)
        new[at, :] = edge_tail(1, before[at, :], latest, w_s, w_o, norms, edge[at, :])

    by_rows(new.shape[0], 256, step)
    part[...] = dot(inc[...], new[...]).astype(BF16)


def after_links(
    me,
    one_hot,
    w_s,
    before,
    w_o,
    bias,
    gain,
    shift,
    edge,
    mixed,
    table,
    cells,
    joined,
    o0,
    o1,
    o2,
    o3,
    new,
    held,
):
    senders = dot(one_hot.get()[...], joined[...]).astype(BF16)
    first, start, second, old = (x.get() for x in (w_s, before, w_o, edge))
    norms = bias.get(), gain.get(), shift.get()
    new[...] = edge_tail(2, start[...], senders, first, second, norms, old[...])
    links, count = new.shape[0], held.shape[0]
    low = 3 * lax.broadcasted_iota(jnp.int32, (count, links), 0)
    column = lax.broadcasted_iota(jnp.int32, (count, links), 1)
    added = dot(mask((column >= low) & (column < low + 3)), new[...]).astype(BF16)
    rows, weights, latent = table.get(), mixed.get(), cells.get()[...]
    pre = rows[4:5, :] + dot(latent, weights[0:512, :])
    held[...] = node_tail(2, latent, pre, added, weights, rows)
    for k, out in enumerate((o0, o1, o2, o3)):
        out[...] = held[:, lanes(lax.rem(me[0] + k, 4))]


def sum_body(s0, s1, s2, s3, one_hot, summed, outgoing):
    total = s0[...].astype(F32) + s1[...].astype(F32) + s2[...].astype(F32) + s3[...].astype(F32)
    summed[...] = total.astype(BF16)
    outgoing[...] = dot(one_hot[...], summed[...]).astype(BF16)


def node_first(me, latent, mixed, table, s0, s1, s2, s3, new, summed):
    for k, tile in enumerate((s0, s1, s2, s3)):
        summed[:, lanes(owner(me, k))] = tile[...]
    old = latent.get()

    def step(at):
        pre = table[0:1, :] + dot(old[at, :], mixed[0:512, :])
        new[at, :] = node_tail(0, old[at, :], pre, summed[at, :], mixed, table)

    by_rows(new.shape[0], 128, step)


def node_second(latent, mixed, table, p0, p1, p2, p3, one_hot, outgoing, new):
    total = p0[...].astype(F32) + p1[...].astype(F32) + p2[...].astype(F32) + p3[...].astype(F32)
    old = latent[...]
    pre = table[2:3, :] + dot(old, mixed[0:512, :])
    new[...] = node_tail(1, old, pre, total.astype(BF16), mixed, table)
    outgoing[...] = dot(one_hot[...], new[...]).astype(BF16)


def join_body(me, r0, r1, r2, r3, out, sems):
    copies = []
    for k, tile in enumerate((r0, r1, r2, r3)):
        height = tile.shape[0]
        target = out.at[rows_at(owner(me, k), height)]
        copies.append(pltpu.make_async_copy(tile, target, sems.at[k]))
    for copy in copies:
        copy.start()
    for copy in copies:
        copy.wait()


def moved(x, shift):
    return lax.ppermute(x, "feat", [(i, (i + shift) % 4) for i in range(4)])


def around(x):
    three, two, one = (moved(x, k) for k in (3, 2, 1))
    return [x, one, two, three]


def handed(pieces):
    three, two, one = (moved(pieces[k], k) for k in (3, 2, 1))
    return [pieces[0], one, two, three]


def from_neighbours(whole, half):
    size = lax.axis_size("node")
    ring = [
        (n * 4 + f, n * 4 + (f + (1 if n % 2 == 0 else 3)) % 4) for n in range(size) for f in range(4)
    ]
    return lax.ppermute(whole, ("node", "feat"), ring), moved(half, 2)


def from_twin(x):
    return lax.ppermute(x, "node", [(n, n ^ 1) for n in range(lax.axis_size("node"))])


def over_nodes(x, blocks):
    tiles = x.reshape(blocks, x.shape[0] // blocks, x.shape[1])
    return lax.all_to_all(tiles, "node", split_axis=0, concat_axis=0, tiled=True).reshape(x.shape)


together = lax.optimization_barrier


def local(
    mesh_nodes,
    mesh_edges,
    grid_nodes,
    m2g_edges,
    edge_receivers,
    edge_slots,
    send_rows,
    m2g_slots,
    m2g_send_rows,
    edge_w_in,
    edge_w_out,
    edge_bias,
    edge_gain,
    edge_shift,
    node_w_in,
    node_w_out,
    node_bias,
    node_gain,
    node_shift,
):
    who = jnp.stack([lax.axis_index("feat"), lax.rem(lax.axis_index("node"), 2)]).astype(jnp.int32)
    nodes, share = mesh_nodes.shape
    edges, width = mesh_edges.shape
    links = m2g_edges.shape[0]
    blocks, slot = send_rows.shape[1:]
    slots = blocks * slot
    cells = grid_nodes.shape[0] // 4
    square = 2 * width * width
    rows, link_rows = send_rows[0].T, m2g_send_rows[0].T
    norms = [(edge_bias, ()), (edge_gain, ()), (edge_shift, ())]
    slot_row, receiver_row = edge_slots.reshape(1, edges), edge_receivers.reshape(1, edges)

    (outgoing,) = call(
        first_gather,
        far=[(rows, ()), (mesh_nodes, ())],
        outs=[shape((slots, share))],
        scratch=[pltpu.VMEM((slots, nodes), BF16)],
    )
    outgoing, late_nodes, late_who = together((outgoing, mesh_nodes, who))
    arrived = over_nodes(outgoing, blocks)
    node_tiles = around(late_nodes)
    prepared = setup(late_who, node_w_in, node_w_out, node_bias, node_gain, node_shift, grid_nodes)
    whole, half, whole_2, half_2, *grid_pieces = prepared
    arrived, half = together((arrived, half))
    tiles = around(arrived)
    latent, held, oh_s, inc, oh_o, w_s, w_o, edge = call(
        before_first,
        me=who,
        far=[(edge_w_in, (0, 0)), (edge_w_in, (0, 2)), (edge_bias, ())],
        passed=[(edge_w_in, (0, 1)), (edge_w_out, (0,)), (mesh_edges, ())],
        near=[*node_tiles, slot_row, receiver_row, rows],
        kept=[shape((nodes, width))],
        outs=[
            shape((edges, width), F32),
            shape((edges, slots)),
            shape((nodes, edges)),
            shape((slots, nodes)),
        ],
        scratch=[pltpu.VMEM((edges, nodes), BF16)],
        flops=2 * edges * square,
    )
    pair = [pltpu.VMEM((slots, 2 * share), BF16), pltpu.VMEM((2 * share, width), BF16)]
    held, early = call(
        early_first,
        me=who,
        near=[held, oh_s, w_s, tiles[0], tiles[2]],
        outs=[shape((edges, width), F32), shape((edges, 2 * share))],
        scratch=pair,
        flops=edges * square,
    )
    edge, senders, *partial = call(
        after_first,
        me=who,
        far=norms,
        near=[held, early, oh_s, w_s, w_o, edge, tiles[1], tiles[3], inc],
        kept=[shape((edges, width)), shape((edges, width))],
        outs=[shape((nodes, share))] * 4,
        scratch=[*pair, pltpu.VMEM((nodes, width), BF16)],
        flops=4 * edges * square,
    )
    *partial, whole, half = together((*partial, whole, half))
    sums = handed(partial)
    near, far = from_neighbours(whole, half)
    summed, outgoing = call(
        sum_body,
        near=[*sums, oh_o],
        outs=[shape((nodes, share)), shape((slots, share))],
        flops=2 * slots * nodes * share,
    )

    outgoing, summed = together((outgoing, summed))
    arrived = over_nodes(outgoing, blocks)
    sum_tiles = around(summed)
    twins = from_twin(near), from_twin(far)
    tiles = around(arrived)
    far_table, mixed_0, mixed_1, table = call(
        weights_first,
        me=who,
        near=[whole, near, twins[0], far, twins[1]],
        kept=[shape((16, width), F32)],
        outs=[shape((3 * width, width))] * 2 + [shape((16, width), F32)],
        scratch=[pltpu.VMEM(whole.shape, BF16)],
    )
    (latent,) = call(
        node_first,
        me=who,
        far=[(latent, ())],
        near=[mixed_0, table, *sum_tiles],
        outs=[shape((nodes, width))],
        scratch=[pltpu.VMEM((nodes, width), BF16)],
        flops=3 * nodes * square,
    )
    held, sender_pre, oh_s, inc, oh_o, w_s, w_o, edge, senders = call(
        before_second,
        far=[(edge_w_in, (1, 0)), (edge_w_in, (1, 2)), (edge_bias, ())],
        passed=[(edge_w_in, (1, 1)), (edge_w_out, (1,)), (edge, ()), (senders, ())],
        near=[latent, mixed_0, table, slot_row, receiver_row, link_rows],
        outs=[
            shape((edges, width), F32),
            shape((edges, width), F32),
            shape((edges, slots)),
            shape((nodes, edges)),
            shape((slots, nodes)),
        ],
        scratch=[pltpu.VMEM((edges, nodes), BF16)],
        flops=3 * edges * square,
    )
    (sender_pre,) = call(
        early_second,
        me=who,
        near=[sender_pre, oh_s, mixed_0, tiles[0], tiles[2]],
        outs=[shape((edges, width), F32)],
        scratch=pair,
        flops=edges * square,
    )
    (part,) = call(
        after_second,
        me=who,
        far=norms,
        near=[held, sender_pre, oh_s, w_s, w_o, edge, senders, mixed_0, table, tiles[1], tiles[3], inc],
        outs=[shape((nodes, width))],
        scratch=[*pair, pltpu.VMEM((edges, width), BF16)],
        flops=6 * edges * square,
    )
    parts = around(part)
    (outgoing,) = call(
        node_second,
        near=[latent, mixed_1, table, *parts, oh_o],
        outs=[shape((slots, width))],
        scratch=[pltpu.VMEM((nodes, width), BF16)],
        flops=3 * nodes * square,
    )

    outgoing, whole_2, half_2, *grid_pieces = together((outgoing, whole_2, half_2, *grid_pieces))
    arrived = over_nodes(outgoing, blocks)
    near, far = from_neighbours(whole_2, half_2)
    grid_tiles = handed(grid_pieces)
    twins = from_twin(near), from_twin(far)
    (mixed_2,) = call(
        weights_last,
        me=who,
        near=[whole_2, near, twins[0], far, twins[1]],
        kept=[shape((3 * width, width))],
        scratch=[pltpu.VMEM(whole_2.shape, BF16)],
    )
    held, whole_cells, oh_m = call(
        before_links,
        me=who,
        far=[
            (edge_w_in, (2, 0)),
            (edge_w_in, (2, 2)),
            (edge_bias, ()),
            (m2g_edges, ()),
        ],
        near=[*grid_tiles, m2g_slots.reshape(1, links)],
        kept=[shape((links, width), F32), shape((cells, width)), shape((links, slots))],
        scratch=[pltpu.VMEM((links, cells), BF16)],
        flops=2 * links * square,
    )
    arrived, held, mixed_2 = together((arrived, held, mixed_2))
    pieces = call(
        after_links,
        me=who,
        far=[
            (oh_m, ()),
            (edge_w_in, (2, 1)),
            (held, ()),
            (edge_w_out, (2,)),
            *norms,
            (m2g_edges, ()),
            (mixed_2, ()),
            (far_table, ()),
            (whole_cells, ()),
        ],
        near=[arrived],
        outs=[shape((cells, share))] * 4,
        scratch=[pltpu.VMEM((links, width), BF16), pltpu.VMEM((cells, width), BF16)],
        flops=8 * links * square,
    )
    pieces = handed(pieces)
    return pl.pallas_call(
        join_body,
        out_shape=shape((4 * cells, share)),
        in_specs=[SMEM] + [pl.BlockSpec(memory_space=pl.ANY)] * 4,
        out_specs=pl.BlockSpec(memory_space=pl.ANY),
        scratch_shapes=[pltpu.SemaphoreType.DMA((4,))],
        name="join",
        compiler_params=pltpu.CompilerParams(vmem_limit_bytes=20 << 20),
    )(who, *pieces)


def solution(mesh):
    in_specs = (
        P("node", "feat"),
        P(("node", "feat"), None),
        P("node", "feat"),
        P(("node", "feat"), None),
        P(("node", "feat")),
        P(("node", "feat")),
        P("node", None, None),
        P(("node", "feat")),
        P("node", None, None),
        P(),
        P(),
        P(),
        P(),
        P(),
        P(None, None, "feat", None),
        P(None, "feat", None),
        P(None, None, "feat"),
        P(None, "feat"),
        P(None, "feat"),
    )
    out_specs = P("node", "feat")

    return jax.shard_map(local, mesh=mesh, in_specs=in_specs, out_specs=out_specs, check_vma=False)
```
